32 devices in a mesh: coarse: 8 (over z, y), fine: 4 (over x, core).
Axes of the slice: x: 2, y: 2, z: 4, core: 2. Of those that a mesh axis runs over, the one named last changes fastest.
Arguments:
- right_side: float32 [64, 32, 128], P('coarse', 'fine'), may hold values from -6 to 6
- coefficient_index: int32 [64, 32, 128], P('coarse', 'fine'), may hold values from 0 to 15
- material_coefficients: float32 [16], replicated, may hold values from 0.02 to 0.5
- block_cells: int32 [8, 4, 64, 128], P('coarse', 'fine'), may hold values from 0 to 8191, as said below
- block_inverses: float32 [8, 4, 64, 128, 128], P('coarse', 'fine'), as said below
- aggregate_map: int32 [64, 32, 128], P('coarse', 'fine'), may hold values from 0 to 15, as said below
- coarse_diagonal: float32 [8, 4, 16], P('coarse', 'fine'), may hold values from 0.1 to 8
Outputs:
- solution: float32 [64, 32, 128], P('coarse', 'fine')
- residual: float32 [64, 32, 128], P('coarse', 'fine')
- direction: float32 [64, 32, 128], P('coarse', 'fine')
The draws below stay inside these ranges and needn't reach their ends.
Inputs may be any that keep to these rules, and one draw needn't show every extreme that they name: `block_cells`: each device block's 64 x 128 entries list each of its local cell numbers exactly once. `block_inverses`: every 128 x 128 matrix is symmetric positive definite. A cell with third index j has aggregate_map equal to j // 8 - 1, j // 8 or j // 8 + 1.
All inputs are finite; a program needn't handle non-finite values.
Results may differ from the reference program's by a relative error of at most 0.00016.
Values sent between devices are 32-bit elements; how exact they have to be, the bound alone decides.
A program may use at most 64 MiB of HBM per device.

```python
import math
import jax
import jax.numpy as jnp
from jax import lax

AGG = 8
NY = 128
BS = 128
MATERIALS = 16
ITERS = 2
SWEEPS = 4
OWNERS = 8
MEMBERS = 4
NX = 64
NZ = 32
MY = 16
NBLK = 64


def draw_right_side(key, part):
    first = jax.random.fold_in(key, 0)
    xs = jnp.arange(NX, dtype=jnp.float32)[:, None, None]
    zs = jnp.arange(NZ, dtype=jnp.float32)[None, :, None]
    scale = 0.6 + 1.2 * (xs + zs) / (NX + NZ - 2)
    rough = jnp.clip(jax.random.normal(first, (NX, NZ, NY), jnp.float32), -3.3, 3.3)
    return rough * scale


def draw_aggregate_map(key, part):
    ys = jnp.arange(NY, dtype=jnp.int32)[None, None, :]
    moves = jax.random.randint(key, (NX, NZ, NY), -3, 4, dtype=jnp.int32)
    return jnp.clip(ys + moves, 0, NY - 1) // AGG


def draw_block_cells(key, part):
    keys = jax.random.split(key, OWNERS * MEMBERS)
    cells = AGG * AGG * NY

    def one_device(single):
        return jax.random.permutation(single, cells)
    orders = jax.vmap(one_device)(keys)
    return orders.astype(jnp.int32).reshape(OWNERS, MEMBERS, NBLK, BS)


def draw_block_inverses(key, part):
    spread, lowest, highest = (0.3, 0.3, 3.0)

    def one_owner(owner):
        base = jax.random.fold_in(key, owner)
        left, right = jax.random.split(base)
        noise = jax.random.normal(left, (MEMBERS, NBLK, BS, BS), jnp.float32) * (spread / math.sqrt(2.0 * BS))
        eye = jnp.eye(BS, dtype=jnp.float32)
        symmetric = (noise + jnp.swapaxes(noise, -1, -2)) * (1.0 - eye)
        scales = jnp.exp(jax.random.uniform(right, (MEMBERS, NBLK, BS), jnp.float32, math.log(lowest), math.log(highest)))
        root = jnp.sqrt(scales)
        return (eye + symmetric) * root[..., :, None] * root[..., None, :]
    return lax.map(one_owner, jnp.arange(OWNERS, dtype=jnp.int32))


def touch_ends(values, stream_key, least, top_value):
    longest = values.shape.index(max(values.shape))
    spots = []
    for shift in (0, 1):
        where = [jax.random.randint(jax.random.fold_in(stream_key, axis), (), 0, length) for axis, length in enumerate(values.shape)]
        where[longest] = (where[longest] + shift) % values.shape[longest]
        spots.append(tuple(where))
    return values.at[spots[0]].set(least).at[spots[1]].set(top_value)


def block_scale(rng, shape, shards, least, top_value):
    loudness = 1.0
    for position, blocks in shards:
        steps = jax.random.uniform(jax.random.fold_in(jax.random.fold_in(rng, 6), position), (blocks,), jnp.float32, least / len(shards), top_value / len(shards))
        loudness = loudness * jnp.repeat(jnp.exp(steps), shape[position] // blocks).reshape((-1,) + (1,) * (len(shape) - 1 - position))
    return loudness


def setup_inputs(seed: int = 0) -> dict:
    arg_keys = jax.random.split(jax.random.key(seed), 8)
    return {
        "right_side": draw_right_side(jax.random.fold_in(arg_keys[7], 71), 0),
        "coefficient_index": touch_ends(jax.random.randint(arg_keys[1], (NX, NZ, NY), 0, MATERIALS), jax.random.fold_in(arg_keys[1], 1), 0, MATERIALS - 1).astype(jnp.int32),
        "material_coefficients": jnp.clip(jnp.exp(jax.random.uniform(arg_keys[2], (MATERIALS,), jnp.float32, math.log(0.02), math.log(0.5))), 0.02, 0.5),
        "block_cells": draw_block_cells(jax.random.fold_in(arg_keys[7], 71), 0),
        "block_inverses": draw_block_inverses(jax.random.fold_in(arg_keys[7], 71), 0),
        "aggregate_map": draw_aggregate_map(jax.random.fold_in(arg_keys[7], 71), 0),
        "coarse_diagonal": jnp.clip(jnp.exp(math.log(8.0) - 4.3820266 * jax.random.uniform(arg_keys[6], (OWNERS, MEMBERS, MY), jnp.float32) ** block_scale(arg_keys[6], (OWNERS, MEMBERS, MY), ((0, 8), (1, 4)), -0.2, 0.2)), 0.1, 8.0),
    }


omega = 0.8
restrict_scale = 0.25


def neighbours():
    result = []
    for shift_x in (-1, 0, 1):
        for shift_z in (-1, 0, 1):
            for shift_y in (-1, 0, 1):
                reach = abs(shift_x) + abs(shift_z) + abs(shift_y)
                if reach > 0:
                    result.append((shift_x, shift_z, shift_y, 0.5 ** (reach - 1)))
    return result


def window(padded, shift_x, shift_z, shift_y, shape):
    return padded[1 + shift_x:1 + shift_x + shape[0], 1 + shift_z:1 + shift_z + shape[1], 1 + shift_y:1 + shift_y + shape[2]]


def fine_operate(field, kappa):
    padded = jnp.pad(field, 1)
    kappa_wide = jnp.pad(kappa, 1)
    total = jnp.zeros(field.shape, jnp.float32)
    for shift_x, shift_z, shift_y, weight in neighbours():
        near_field = window(padded, shift_x, shift_z, shift_y, field.shape)
        near_kappa = window(kappa_wide, shift_x, shift_z, shift_y, field.shape)
        total = total + (weight * 0.5) * (kappa + near_kappa) * (field - near_field)
    return total


def to_local(field):
    return field.reshape(OWNERS, AGG, MEMBERS, AGG, NY).transpose(0, 2, 1, 3, 4).reshape(OWNERS * MEMBERS, AGG * AGG * NY)


def from_local(flat):
    return flat.reshape(OWNERS, MEMBERS, AGG, AGG, NY).transpose(0, 2, 1, 3, 4).reshape(OWNERS * AGG, MEMBERS * AGG, NY)


def block_apply(residual, block_inverses, block_cells):
    local = to_local(residual)
    orders = block_cells.reshape(OWNERS * MEMBERS, NBLK, BS)
    matrices = block_inverses.reshape(OWNERS * MEMBERS, NBLK, BS, BS)

    def one_device(items):
        vector, order, matrix = items
        picked = vector[order]
        product = jnp.einsum("bij,bj->bi", matrix, picked, precision=lax.Precision.HIGHEST)
        return jnp.zeros(vector.shape, jnp.float32).at[order.reshape(-1)].set(product.reshape(-1))

    return from_local(lax.map(one_device, (local, orders, matrices)))


def segment_numbers(aggregate_map):
    base = jnp.arange(OWNERS * MEMBERS, dtype=jnp.int32) * MY
    return to_local(aggregate_map) + base[:, None]


def coarse_operate(guess, diagonal):
    padded = jnp.pad(guess, 1)
    beside = padded[2:, 1:-1, 1:-1] + padded[:-2, 1:-1, 1:-1]
    beside = beside + padded[1:-1, 2:, 1:-1] + padded[1:-1, :-2, 1:-1]
    beside = beside + padded[1:-1, 1:-1, 2:] + padded[1:-1, 1:-1, :-2]
    return (6.0 + diagonal) * guess - beside


def precondition(residual, block_inverses, block_cells, segments, coarse_diagonal):
    smoothed = block_apply(residual, block_inverses, block_cells)
    sums = jax.ops.segment_sum(to_local(residual).reshape(-1), segments.reshape(-1), num_segments=OWNERS * MEMBERS * MY)
    source = restrict_scale * sums.reshape(OWNERS, MEMBERS, MY)
    guess = jnp.zeros(source.shape, jnp.float32)
    for sweep in range(SWEEPS):
        guess = guess + omega * (source - coarse_operate(guess, coarse_diagonal)) / (6.0 + coarse_diagonal)
    correction = from_local(guess.reshape(-1)[segments])
    return smoothed + correction


def reference(right_side, coefficient_index, material_coefficients, block_cells, block_inverses, aggregate_map, coarse_diagonal):
    kappa = material_coefficients[coefficient_index]
    segments = segment_numbers(aggregate_map)
    solution = jnp.zeros(right_side.shape, jnp.float32)
    residual = right_side
    smoothed = precondition(residual, block_inverses, block_cells, segments, coarse_diagonal)
    current = jnp.sum(residual * smoothed)
    search = smoothed
    for step in range(ITERS):
        image = fine_operate(search, kappa)
        alpha = current / jnp.sum(search * image)
        solution = solution + alpha * search
        residual = residual - alpha * image
        smoothed = precondition(residual, block_inverses, block_cells, segments, coarse_diagonal)
        following = jnp.sum(residual * smoothed)
        search = smoothed + (following / current) * search
        current = following
    return solution, residual, search
```

```python
import functools

import jax
import jax.numpy as jnp
from jax import lax
from jax.experimental import pallas as pl
from jax.experimental.pallas import tpu as pltpu
from jax.sharding import PartitionSpec as P

ITERS = 2
SWEEPS = 4
omega = 0.8
restrict_scale = 0.25
MESH = pl.DeviceIdType.MESH
SUB = 8
LANES = 128
MAIN = 8
XLO, XHI, ZLO, ZHI, CORNER = 8, 9, 10, 11, 12
SLOTS = 13
DIRECTIONS = ((-1, 0), (1, 0), (0, -1), (0, 1), (-1, -1), (-1, 1), (1, -1), (1, 1))


def take(values, lanes):
    return jnp.take_along_axis(values, lanes, axis=1, mode="promise_in_bounds")


def full(row):
    return jnp.broadcast_to(row, (SUB, LANES))


def total_of(values):
    return jnp.sum(jnp.sum(values, axis=0, keepdims=True), axis=1, keepdims=True)


def kernel(
    owners, members, r_ref, cidx_ref, table_ref, cells_ref, inv_ref, amap_ref, diag_ref,
    x_out, r_out, p_out,
    mats, rot, key_in, lane_in, key_out, lane_out, moved,
    first_ext, first_cols, first_corner_src, first_corners,
    later_ext, later_cols, later_corner_src, later_corners,
    kap, amaps, w_ext, p_ext, r_cur, q_cur, kt, small,
    row_src, rows,
    mat_sems, send_sems, recv_sems, row_send, row_recv,
):
    count = owners * members
    o = lax.axis_index("coarse")
    m = lax.axis_index("fine")
    me = o * members + m
    groups = cells_ref.shape[0]
    sub = lax.broadcasted_iota(jnp.int32, (SUB, LANES), 0)
    lane = lax.broadcasted_iota(jnp.int32, (SUB, LANES), 1)
    zero = jnp.zeros((SUB, LANES), jnp.float32)

    mat_copies = [
        pltpu.make_async_copy(
            inv_ref.at[pl.ds(u * SUB, SUB)], mats.at[pl.ds(u * SUB, SUB)], mat_sems.at[u]
        )
        for u in range(groups)
    ]
    for copy in mat_copies:
        copy.start()

    for slot in range(MAIN, CORNER):
        for f in range(3):
            first_ext[slot, f] = zero
        later_ext[slot, 0] = zero
    for c in range(4):
        first_corners[c] = zero
        later_corners[c] = zero

    barrier = pltpu.get_barrier_semaphore()

    def other(d):
        t = lax.rem(me + d, count)
        return {"coarse": lax.div(t, members), "fine": lax.rem(t, members)}

    def announce(d, carry):
        pl.semaphore_signal(barrier, inc=1, device_id=other(d), device_id_type=MESH)
        return carry

    lax.fori_loop(1, count, announce, 0)

    def keys_of(source):
        row = lax.shift_right_logical(source, 7)
        turn = (jnp.bitwise_and(row, 7) - sub) & 7
        return jnp.bitwise_and(row, ~7) + turn, jnp.bitwise_and(source, 127)

    for g in range(groups):
        key, lanes = keys_of(cells_ref[g])
        key_in[g] = key
        lane_in[g] = lanes

    def load_turns(values):
        for g in range(len(values)):
            for turn in range(SUB):
                rot[g * SUB + turn] = (
                    values[g] if turn == 0 else pltpu.roll(values[g], SUB - turn, 0)
                )

    def permuted(key, lanes):
        parts = [zero, zero]
        for k in range(groups * SUB):
            parts[k % 2] = jnp.where(key == k, take(rot[k], lanes), parts[k % 2])
        return parts[0] + parts[1]

    tall = lax.broadcasted_iota(jnp.int32, (groups * SUB, LANES), 0)
    taller = lax.broadcasted_iota(jnp.int32, (LANES, LANES), 0)
    wide = lax.broadcasted_iota(jnp.int32, (groups * SUB, LANES), 1).astype(jnp.float32)

    def find(g, carry):
        block = cells_ref[g]
        for b in range(SUB):
            source = block[b : b + 1, :]
            hit = tall == jnp.broadcast_to(lax.shift_right_logical(source, 7), tall.shape)
            number = (g * SUB + b).astype(jnp.float32)
            left = jnp.concatenate(
                [jnp.where(hit, number, 0.0), jnp.where(hit, wide, 0.0)], axis=0
            ).astype(jnp.bfloat16)
            right = jnp.where(
                taller == jnp.broadcast_to(jnp.bitwise_and(source, 127), taller.shape), 1.0, 0.0
            ).astype(jnp.bfloat16)
            carry = carry + lax.dot_general(
                left, right, (((1,), (1,)), ((), ())), preferred_element_type=jnp.float32
            )
        return carry

    found = lax.fori_loop(
        0, groups, find, jnp.zeros((2 * groups * SUB, LANES), jnp.float32)
    ).astype(jnp.int32)
    for g in range(groups):
        block = found[g * SUB : (g + 1) * SUB]
        place = found[(groups + g) * SUB : (groups + g + 1) * SUB]
        key, lanes = keys_of(block * LANES + place)
        key_out[g] = key
        lane_out[g] = lanes

    small[...] = jnp.zeros(small.shape, jnp.float32)
    small[0, 0:1, 0 : table_ref.shape[1]] = table_ref[...]
    small[1, 0:1, 0 : diag_ref.shape[2]] = diag_ref[0]
    boxes = diag_ref.shape[2]
    table = full(small[0, 0:1, :])
    for x in range(MAIN):
        first_ext[x, 1] = take(table, cidx_ref[x])
        first_ext[x, 2] = (amap_ref[x] + 1).astype(jnp.float32)
        amaps[x] = amap_ref[x]

    spread_sub = lax.shift_right_logical(lane, 4)
    spread_key = (spread_sub - sub) & 7
    spread_lane = (lane & 15) * 8 + sub

    def block_apply(values, done_with_dot):
        load_turns(values)

        def one(u, dot):
            picked = permuted(key_in[u], lane_in[u])
            columns = zero
            for turn in range(SUB):
                turned = picked if turn == 0 else pltpu.roll(picked, SUB - turn, 0)
                columns = jnp.where(spread_key == turn, take(turned, spread_lane), columns)
            product = zero
            for b in range(SUB):
                parts = [None, None]
                for j in range(LANES // SUB):
                    at = b * (LANES // SUB) + j
                    term = mats[u * SUB + b, pl.ds(j * SUB, SUB), :] * jnp.broadcast_to(
                        columns[:, at : at + 1], (SUB, LANES)
                    )
                    parts[j % 2] = term if parts[j % 2] is None else parts[j % 2] + term
                line = jnp.sum(parts[0] + parts[1], axis=0, keepdims=True)
                product = jnp.where(sub == b, full(line), product)
            moved[u] = product
            return dot + picked * product

        dot = lax.fori_loop(0, groups, one, zero)
        done_with_dot(total_of(dot))
        load_turns([moved[g] for g in range(groups)])

        def back(g, carry):
            moved[g] = permuted(key_out[g], lane_out[g])
            return carry

        lax.fori_loop(0, groups, back, 0)
        return [moved[g] for g in range(groups)]

    base = lax.shift_right_logical(lane, 3)

    def restrict(values):
        sums = []
        for move in (-1, 0, 1):
            total = zero
            for x in range(MAIN):
                total = total + jnp.where(amaps[x] - base == move, values[x], 0.0)
            sums.append(total)
        total = pltpu.roll(sums[0], LANES - SUB, 1) + sums[1] + pltpu.roll(sums[2], SUB, 1)
        total = full(jnp.sum(total, axis=0, keepdims=True))
        for step in (1, 2, 4):
            total = total + pltpu.roll(total, LANES - step, 1)
        return jnp.where(lane < boxes, restrict_scale * take(total, (lane * SUB) & 127), 0.0)

    def row_copy(index, src, dst, device):
        return pltpu.make_async_remote_copy(
            src_ref=src, dst_ref=dst, send_sem=row_send.at[index], recv_sem=row_recv.at[index],
            device_id=device, device_id_type=MESH,
        )

    def send_rows(index, row):
        row_src[index] = row[0:1, :]
        rows[index, me] = row[0:1, :]

        def one(d, carry):
            row_copy(index, row_src.at[index], rows.at[index, me], other(d)).start()
            return carry

        lax.fori_loop(1, count, one, 0)

    def wait_rows(index):
        part = rows.at[index, pl.ds(0, count - 1)]
        both = row_copy(index, part, part, other(1))
        both.wait_send()
        both.wait_recv()
        return rows[index].reshape(count, LANES)

    def scalar(row, number):
        at = 2 * boxes + number
        return row[:, at : at + 1]

    def with_scalar(row, number, value):
        return jnp.where(lane == 2 * boxes + number, full(value), row)

    def edge_rows(values, z):
        result = zero
        for x in range(MAIN):
            result = jnp.where(sub == x, full(values[x][z : z + 1, :]), result)
        return result

    def halo_copies(ring, ext, cols, corner_src, corners):
        copies = []
        for number, (do, dm) in enumerate(DIRECTIONS):
            if dm == 0:
                src = ext.at[MAIN - 1 if do == 1 else 0]
                dst = ext.at[XLO if do == 1 else XHI]
            elif do == 0:
                src = cols.at[1 if dm == 1 else 0]
                dst = ext.at[ZLO if dm == 1 else ZHI]
            else:
                at = 2 * (0 if do == 1 else 1) + (0 if dm == 1 else 1)
                src = corner_src.at[at]
                dst = corners.at[at]
            to_o, to_m = o + do, m + dm
            from_o, from_m = o - do, m - dm
            goes = (to_o >= 0) & (to_o < owners) & (to_m >= 0) & (to_m < members)
            comes = (from_o >= 0) & (from_o < owners) & (from_m >= 0) & (from_m < members)
            copies.append(
                (
                    goes,
                    comes,
                    pltpu.make_async_remote_copy(
                        src_ref=src, dst_ref=dst,
                        send_sem=send_sems.at[ring, number], recv_sem=recv_sems.at[ring, number],
                        device_id={"coarse": to_o, "fine": to_m}, device_id_type=MESH,
                    ),
                )
            )
        return copies

    def start_halo(ring, fields, ext, cols, corner_src, corners):
        packs = [zero, zero, zero, zero]
        for f, values in enumerate(fields):
            cols[0, f] = edge_rows(values, 0)
            cols[1, f] = edge_rows(values, SUB - 1)
            for side_x in range(2):
                for side_z in range(2):
                    at = 2 * side_x + side_z
                    x = MAIN - 1 if side_x == 0 else 0
                    z = SUB - 1 if side_z == 0 else 0
                    packs[at] = jnp.where(sub == f, full(values[x][z : z + 1, :]), packs[at])
        for at in range(4):
            corner_src[at] = packs[at]
        copies = halo_copies(ring, ext, cols, corner_src, corners)
        for goes, _, copy in copies:
            pl.when(goes)(copy.start)
        return copies

    def wait_halo(copies):
        for goes, comes, copy in copies:
            pl.when(goes)(copy.wait_send)
            pl.when(comes)(copy.wait_recv)

    def corner_rows(corners, f):
        result = zero
        for at in range(4):
            result = jnp.where(sub == at, full(corners[at][f : f + 1, :]), result)
        return result

    def shifted(values, low, high):
        before = jnp.where(sub == 0, full(low), pltpu.roll(values, 1, 0))
        after = jnp.where(sub == SUB - 1, full(high), pltpu.roll(values, SUB - 1, 0))
        return values + 0.5 * (before + after)

    def smear(v):
        planes = [v[XLO]] + [v[x] for x in range(MAIN)] + [v[XHI]]
        corner = v[CORNER]
        low = shifted(v[ZLO], corner[0:1, :], corner[2:3, :])
        high = shifted(v[ZHI], corner[1:2, :], corner[3:4, :])
        result = []
        for x in range(MAIN):
            mid = planes[x + 1] + 0.5 * (planes[x] + planes[x + 2])
            mid = shifted(mid, low[x : x + 1, :], high[x : x + 1, :])
            before = jnp.where(lane == 0, 0.0, pltpu.roll(mid, 1, 1))
            after = jnp.where(lane == LANES - 1, 0.0, pltpu.roll(mid, LANES - 1, 1))
            result.append(mid + 0.5 * (before + after))
        return result

    node = lax.broadcasted_iota(jnp.int32, (count, LANES), 0)
    node_lane = lax.broadcasted_iota(jnp.int32, (count, LANES), 1)
    member = lax.rem(node, members)

    def coarse_solve(source, inverse):
        guess = omega * source * inverse
        for sweep in range(SWEEPS - 1):
            beside = pltpu.roll(guess, 1, 1) + pltpu.roll(guess, LANES - 1, 1)
            beside = beside + jnp.where(member == 0, 0.0, pltpu.roll(guess, 1, 0))
            beside = beside + jnp.where(
                member == members - 1, 0.0, pltpu.roll(guess, count - 1, 0)
            )
            beside = beside + jnp.where(node < members, 0.0, pltpu.roll(guess, members, 0))
            beside = beside + jnp.where(
                node >= count - members, 0.0, pltpu.roll(guess, count - members, 0)
            )
            guess = (1.0 - omega) * guess + omega * (source + beside) * inverse
        return guess

    def prolonged(guess, slot_row):
        return slot_row

    start = [r_ref[x] for x in range(MAIN)]
    first_row = restrict(start) + pltpu.roll(full(small[1, 0:1, :]), boxes, 1)
    for copy in mat_copies:
        copy.wait()

    def first_send(dot):
        pl.semaphore_wait(barrier, count - 1)
        send_rows(0, with_scalar(first_row, 0, dot))

    w = block_apply(start, first_send)
    for x in range(MAIN):
        first_ext[x, 0] = w[x]
    kappas = [first_ext[x, 1] for x in range(MAIN)]
    maps = [first_ext[x, 2] for x in range(MAIN)]
    copies = start_halo(
        0, [w, kappas, maps], first_ext, first_cols, first_corner_src, first_corners
    )
    gathered = wait_rows(0)
    diagonal = pltpu.roll(gathered, LANES - boxes, 1)
    inverse = jnp.where(
        node_lane < boxes, 1.0 / jnp.where(node_lane < boxes, 6.0 + diagonal, 1.0), 0.0
    )
    source = jnp.where(node_lane < boxes, gathered, 0.0)
    guess = coarse_solve(source, inverse)
    local_part = scalar(jnp.sum(gathered, axis=0, keepdims=True), 0)
    norm = local_part + total_of(source * guess) * (1.0 / restrict_scale)
    solved = small.shape[0]

    def guess_rows(guess):
        picks = {}
        for do in (-1, 0, 1):
            for dm in (-1, 0, 1):
                wanted = me + do * members + dm
                picks[(do, dm)] = full(
                    jnp.sum(jnp.where(node == wanted, guess, 0.0), axis=0, keepdims=True)
                )
        return picks

    def add_coarse(values, guess):
        picks = guess_rows(guess)
        result = []
        for x in range(MAIN):
            result.append(values[x] + take(picks[(0, 0)], amaps[x]))
        for slot, way in ((XLO, (-1, 0)), (XHI, (1, 0)), (ZLO, (0, -1)), (ZHI, (0, 1))):
            result.append(values[slot] + take(picks[way], amaps[slot]))
        corner = zero
        for at, way in enumerate(((-1, -1), (-1, 1), (1, -1), (1, 1))):
            corner = jnp.where(sub == at, take(picks[way], amaps[CORNER]), corner)
        result.append(values[CORNER] + corner)
        return result

    wait_halo(copies)
    for slot in range(SLOTS):
        if slot == CORNER:
            parts = [corner_rows(first_corners, f) for f in range(3)]
        else:
            parts = [first_ext[slot, f] for f in range(3)]
        w_ext[slot] = parts[0]
        kap[slot] = parts[1]
        if slot >= MAIN:
            amaps[slot] = (parts[2].astype(jnp.int32) + (LANES - 1)) & (LANES - 1)
    smeared = smear([kap[s] for s in range(SLOTS)])
    for x in range(MAIN):
        kt[x] = 8.0 * kap[x] + smeared[x]
        r_cur[x] = r_ref[x]
    z = add_coarse([w_ext[s] for s in range(SLOTS)], guess)
    for slot in range(SLOTS):
        p_ext[slot] = z[slot]

    for step in range(ITERS):
        last = step == ITERS - 1
        p = [p_ext[s] for s in range(SLOTS)]
        flat = smear(p)
        steep = smear([p[s] * kap[s] for s in range(SLOTS)])
        along, across = zero, zero
        for x in range(MAIN):
            q = p[x] * kt[x] - kap[x] * flat[x] - steep[x]
            q_cur[x] = q
            along = along + p[x] * q
            across = across + w_ext[x] * q
        image = [q_cur[x] for x in range(MAIN)]
        row = restrict(image)
        row = with_scalar(row, 0, total_of(along))
        row = with_scalar(row, 1, total_of(across))

        def later_send(dot, row=row, step=step):
            send_rows(1 + step, with_scalar(row, 2, dot))

        bq = block_apply(image, later_send)
        if not last:
            for x in range(MAIN):
                later_ext[x, 0] = bq[x]
            copies = start_halo(
                1 + step, [bq], later_ext, later_cols, later_corner_src, later_corners
            )
        gathered = wait_rows(1 + step)
        sums = jnp.sum(gathered, axis=0, keepdims=True)
        alpha = norm / scalar(sums, 0)
        source = source - alpha * jnp.where(node_lane < boxes, gathered, 0.0)
        guess = coarse_solve(source, inverse)
        local_part = (
            local_part - 2.0 * alpha * scalar(sums, 1) + alpha * alpha * scalar(sums, 2)
        )
        following = local_part + total_of(source * guess) * (1.0 / restrict_scale)
        beta = full(following / norm)
        alpha = full(alpha)
        norm = following
        for x in range(MAIN):
            moved_x = alpha * p_ext[x]
            x_out[x] = moved_x if step == 0 else x_out[x] + moved_x
            r_cur[x] = r_cur[x] - alpha * q_cur[x]
        if not last:
            wait_halo(copies)
            change = [later_ext[s, 0] for s in range(CORNER)] + [corner_rows(later_corners, 0)]
            for slot in range(SLOTS):
                w_ext[slot] = w_ext[slot] - alpha * change[slot]
            z = add_coarse([w_ext[s] for s in range(SLOTS)], guess)
            for slot in range(SLOTS):
                p_ext[slot] = z[slot] + beta * p_ext[slot]
        else:
            own = full(jnp.sum(jnp.where(node == me, guess, 0.0), axis=0, keepdims=True))
            for x in range(MAIN):
                z_x = w_ext[x] - alpha * bq[x] + take(own, amaps[x])
                p_out[x] = z_x + beta * p_ext[x]
                r_out[x] = r_cur[x]


def shards(
    owners, members, right_side, coefficient_index, material_coefficients, block_cells,
    block_inverses, aggregate_map, coarse_diagonal,
):
    blocks, side = block_cells.shape[2], block_cells.shape[3]
    assert right_side.shape == (SUB, SUB, LANES) and side == LANES and blocks == SUB * SUB
    count = owners * members
    groups = blocks // SUB
    field = jax.ShapeDtypeStruct(right_side.shape, jnp.float32)
    vmem = pl.BlockSpec(memory_space=pltpu.VMEM)
    f32, i32 = jnp.float32, jnp.int32
    tile = (SUB, LANES)
    return pl.pallas_call(
        functools.partial(kernel, owners, members),
        out_shape=(field, field, field),
        in_specs=[vmem, vmem, vmem, vmem, pl.BlockSpec(memory_space=pl.ANY), vmem, vmem],
        out_specs=(vmem, vmem, vmem),
        scratch_shapes=[
            pltpu.VMEM((blocks, side, side), f32),
            pltpu.VMEM((blocks,) + tile, f32),
            pltpu.VMEM((groups,) + tile, i32),
            pltpu.VMEM((groups,) + tile, i32),
            pltpu.VMEM((groups,) + tile, i32),
            pltpu.VMEM((groups,) + tile, i32),
            pltpu.VMEM((groups,) + tile, f32),
            pltpu.VMEM((CORNER, 3) + tile, f32),
            pltpu.VMEM((2, 3) + tile, f32),
            pltpu.VMEM((4,) + tile, f32),
            pltpu.VMEM((4,) + tile, f32),
            pltpu.VMEM((CORNER, 1) + tile, f32),
            pltpu.VMEM((2, 1) + tile, f32),
            pltpu.VMEM((4,) + tile, f32),
            pltpu.VMEM((4,) + tile, f32),
            pltpu.VMEM((SLOTS,) + tile, f32),
            pltpu.VMEM((SLOTS,) + tile, i32),
            pltpu.VMEM((SLOTS,) + tile, f32),
            pltpu.VMEM((SLOTS,) + tile, f32),
            pltpu.VMEM((MAIN,) + tile, f32),
            pltpu.VMEM((MAIN,) + tile, f32),
            pltpu.VMEM((MAIN,) + tile, f32),
            pltpu.VMEM((2,) + tile, f32),
            pltpu.VMEM((1 + ITERS, 1, LANES), f32),
            pltpu.VMEM((1 + ITERS, count, 1, LANES), f32),
            pltpu.SemaphoreType.DMA((groups,)),
            pltpu.SemaphoreType.DMA((ITERS, len(DIRECTIONS))),
            pltpu.SemaphoreType.DMA((ITERS, len(DIRECTIONS))),
            pltpu.SemaphoreType.DMA((1 + ITERS,)),
            pltpu.SemaphoreType.DMA((1 + ITERS,)),
        ],
        compiler_params=pltpu.CompilerParams(
            collective_id=0, has_side_effects=True, vmem_limit_bytes=32 << 20
        ),
    )(
        right_side,
        coefficient_index,
        material_coefficients.reshape(1, -1),
        block_cells.reshape(groups, SUB, LANES),
        block_inverses.reshape(blocks, side, side),
        aggregate_map,
        coarse_diagonal,
    )


def solution(mesh):
    three = P("coarse", "fine", None)
    return jax.shard_map(
        functools.partial(shards, mesh.shape["coarse"], mesh.shape["fine"]),
        mesh=mesh,
        in_specs=(
            three,
            three,
            P(),
            P("coarse", "fine", None, None),
            P("coarse", "fine", None, None, None),
            three,
            three,
        ),
        out_specs=(three, three, three),
        check_vma=False,
    )
```

```python
import functools

import jax
import jax.numpy as jnp
from jax import lax
from jax.experimental import pallas as pl
from jax.experimental.pallas import tpu as pltpu
from jax.sharding import PartitionSpec as P

ITERS = 2
SWEEPS = 4
omega = 0.8
restrict_scale = 0.25
MESH = pl.DeviceIdType.MESH
SUB = 8
LANES = 128
MAIN = 8
XLO, XHI, ZLO, ZHI, CORNER = 8, 9, 10, 11, 12
SLOTS = 13
DIRECTIONS = ((-1, 0), (1, 0), (0, -1), (0, 1), (-1, -1), (-1, 1), (1, -1), (1, 1))


def take(values, lanes):
    return jnp.take_along_axis(values, lanes, axis=1, mode="promise_in_bounds")


def full(row):
    return jnp.broadcast_to(row, (SUB, LANES))


def total_of(values):
    return jnp.sum(jnp.sum(values, axis=0, keepdims=True), axis=1, keepdims=True)


def kernel(
    owners, members, r_hbm, cidx_hbm, table_hbm, cells_hbm, inv_ref, amap_hbm, diag_hbm,
    x_out, r_out, p_out,
    r_ref, cidx_ref, table_ref, cells_ref, amap_ref, diag_ref, in_sems,
    mats, halves, rot, key_in, lane_in, key_out, lane_out, moved,
    first_ext, first_cols, first_corner_src, first_corners,
    later_ext, later_cols, later_corner_src, later_corners,
    kap, amaps, w_ext, p_ext, r_cur, q_cur, kt, small,
    row_src, rows,
    mat_sems, send_sems, recv_sems, row_send, row_recv,
):
    count = owners * members
    o = lax.axis_index("coarse")
    m = lax.axis_index("fine")
    me = o * members + m
    groups = cells_ref.shape[0]
    sub = lax.broadcasted_iota(jnp.int32, (SUB, LANES), 0)
    lane = lax.broadcasted_iota(jnp.int32, (SUB, LANES), 1)
    zero = jnp.zeros((SUB, LANES), jnp.float32)

    in_copies = [
        pltpu.make_async_copy(src, dst, in_sems.at[at])
        for at, (src, dst) in enumerate(
            (
                (cells_hbm, cells_ref),
                (r_hbm, r_ref),
                (amap_hbm, amap_ref),
                (cidx_hbm, cidx_ref),
                (table_hbm, table_ref),
                (diag_hbm, diag_ref),
            )
        )
    ]
    for copy in in_copies:
        copy.start()
    def mat_copy(u):
        part = pl.ds(u * SUB, SUB)
        return pltpu.make_async_copy(inv_ref.at[part], mats.at[part], mat_sems.at[u])

    for u in range(groups):
        mat_copy(u).start()

    for slot in range(MAIN, CORNER):
        for f in range(3):
            first_ext[slot, f] = zero
        later_ext[slot, 0] = zero
    for c in range(4):
        first_corners[c] = zero
        later_corners[c] = zero

    barrier = pltpu.get_barrier_semaphore()

    def other(d):
        t = lax.rem(me + d, count)
        return {"coarse": lax.div(t, members), "fine": lax.rem(t, members)}

    def announce(d, carry):
        pl.semaphore_signal(barrier, inc=1, device_id=other(d), device_id_type=MESH)
        return carry

    lax.fori_loop(1, count, announce, 0)

    in_copies[0].wait()

    def keys_of(source):
        row = lax.shift_right_logical(source, 7)
        turn = (jnp.bitwise_and(row, 7) - sub) & 7
        return jnp.bitwise_and(row, ~7) + turn, jnp.bitwise_and(source, 127)

    for g in range(groups):
        key, lanes = keys_of(cells_ref[g])
        key_in[g] = key
        lane_in[g] = lanes

    def load_turns(values):
        for g in range(len(values)):
            for turn in range(SUB):
                rot[g * SUB + turn] = (
                    values[g] if turn == 0 else pltpu.roll(values[g], SUB - turn, 0)
                )

    def permuted(key, lanes):
        parts = [zero, zero]
        for k in range(groups * SUB):
            parts[k % 2] = jnp.where(key == k, take(rot[k], lanes), parts[k % 2])
        return parts[0] + parts[1]

    tall = lax.broadcasted_iota(jnp.int32, (groups * SUB, LANES), 0)
    taller = lax.broadcasted_iota(jnp.int32, (LANES, LANES), 0)
    wide = lax.broadcasted_iota(jnp.int32, (groups * SUB, LANES), 1).astype(jnp.float32)

    def find(g, carry):
        block = cells_ref[g]
        for b in range(SUB):
            source = block[b : b + 1, :]
            hit = tall == jnp.broadcast_to(lax.shift_right_logical(source, 7), tall.shape)
            number = (g * SUB + b).astype(jnp.float32)
            left = jnp.concatenate(
                [jnp.where(hit, number, 0.0), jnp.where(hit, wide, 0.0)], axis=0
            ).astype(jnp.bfloat16)
            right = jnp.where(
                taller == jnp.broadcast_to(jnp.bitwise_and(source, 127), taller.shape), 1.0, 0.0
            ).astype(jnp.bfloat16)
            carry = carry + lax.dot_general(
                left, right, (((1,), (1,)), ((), ())), preferred_element_type=jnp.float32
            )
        return carry

    found = lax.fori_loop(
        0, groups, find, jnp.zeros((2 * groups * SUB, LANES), jnp.float32)
    ).astype(jnp.int32)
    for g in range(groups):
        block = found[g * SUB : (g + 1) * SUB]
        place = found[(groups + g) * SUB : (groups + g + 1) * SUB]
        key, lanes = keys_of(block * LANES + place)
        key_out[g] = key
        lane_out[g] = lanes

    for copy in in_copies[1:]:
        copy.wait()
    small[...] = jnp.zeros(small.shape, jnp.float32)
    small[0, 0:1, 0 : table_ref.shape[1]] = table_ref[...]
    small[1, 0:1, 0 : diag_ref.shape[2]] = diag_ref[0]
    boxes = diag_ref.shape[2]
    table = full(small[0, 0:1, :])
    for x in range(MAIN):
        first_ext[x, 1] = take(table, cidx_ref[x])
        first_ext[x, 2] = (amap_ref[x] + 1).astype(jnp.float32)
        amaps[x] = amap_ref[x]

    def split(values):
        high = values.astype(jnp.bfloat16)
        low = (values - high.astype(jnp.float32)).astype(jnp.bfloat16)
        return high, low

    def block_apply(values, done_with_dot, first=False):
        load_turns(values)

        def one(u, dot):
            if first:
                mat_copy(u).wait()
                for b in range(SUB):
                    high, low = split(mats[u * SUB + b])
                    halves[u * SUB + b, :, 0:LANES] = high
                    halves[u * SUB + b, :, LANES : 2 * LANES] = low
            picked = permuted(key_in[u], lane_in[u])
            left = jnp.concatenate(split(picked), axis=0)
            product = zero
            for b in range(SUB):
                both = jnp.dot(left, halves[u * SUB + b], preferred_element_type=jnp.float32)
                line = both[:SUB, :LANES] + (both[SUB:, :LANES] + both[:SUB, LANES:])
                line = line + both[SUB:, LANES:]
                product = jnp.where(sub == b, line, product)
            moved[u] = product
            return dot + picked * product

        dot = lax.fori_loop(0, groups, one, zero)
        done_with_dot(total_of(dot))
        load_turns([moved[g] for g in range(groups)])

        def back(g, carry):
            moved[g] = permuted(key_out[g], lane_out[g])
            return carry

        lax.fori_loop(0, groups, back, 0)
        return [moved[g] for g in range(groups)]

    base = lax.shift_right_logical(lane, 3)

    def restrict(values):
        sums = []
        for move in (-1, 0, 1):
            total = zero
            for x in range(MAIN):
                total = total + jnp.where(amaps[x] - base == move, values[x], 0.0)
            sums.append(total)
        total = pltpu.roll(sums[0], LANES - SUB, 1) + sums[1] + pltpu.roll(sums[2], SUB, 1)
        total = full(jnp.sum(total, axis=0, keepdims=True))
        for step in (1, 2, 4):
            total = total + pltpu.roll(total, LANES - step, 1)
        return jnp.where(lane < boxes, restrict_scale * take(total, (lane * SUB) & 127), 0.0)

    def row_copy(index, src, dst, device):
        return pltpu.make_async_remote_copy(
            src_ref=src, dst_ref=dst, send_sem=row_send.at[index], recv_sem=row_recv.at[index],
            device_id=device, device_id_type=MESH,
        )

    def send_rows(index, row):
        row_src[index] = row[0:1, :]
        rows[index, me] = row[0:1, :]

        def one(d, carry):
            row_copy(index, row_src.at[index], rows.at[index, me], other(d)).start()
            return carry

        lax.fori_loop(1, count, one, 0)

    def wait_rows(index):
        part = rows.at[index, pl.ds(0, count - 1)]
        both = row_copy(index, part, part, other(1))
        both.wait_send()
        both.wait_recv()
        return rows[index].reshape(count, LANES)

    def scalar(row, number):
        at = 2 * boxes + number
        return row[:, at : at + 1]

    def with_scalar(row, number, value):
        return jnp.where(lane == 2 * boxes + number, full(value), row)

    def edge_rows(values, z):
        result = zero
        for x in range(MAIN):
            result = jnp.where(sub == x, full(values[x][z : z + 1, :]), result)
        return result

    def halo_copies(ring, ext, cols, corner_src, corners):
        copies = []
        for number, (do, dm) in enumerate(DIRECTIONS):
            if dm == 0:
                src = ext.at[MAIN - 1 if do == 1 else 0]
                dst = ext.at[XLO if do == 1 else XHI]
            elif do == 0:
                src = cols.at[1 if dm == 1 else 0]
                dst = ext.at[ZLO if dm == 1 else ZHI]
            else:
                at = 2 * (0 if do == 1 else 1) + (0 if dm == 1 else 1)
                src = corner_src.at[at]
                dst = corners.at[at]
            to_o, to_m = o + do, m + dm
            from_o, from_m = o - do, m - dm
            goes = (to_o >= 0) & (to_o < owners) & (to_m >= 0) & (to_m < members)
            comes = (from_o >= 0) & (from_o < owners) & (from_m >= 0) & (from_m < members)
            copies.append(
                (
                    goes,
                    comes,
                    pltpu.make_async_remote_copy(
                        src_ref=src, dst_ref=dst,
                        send_sem=send_sems.at[ring, number], recv_sem=recv_sems.at[ring, number],
                        device_id={"coarse": to_o, "fine": to_m}, device_id_type=MESH,
                    ),
                )
            )
        return copies

    def start_halo(ring, fields, ext, cols, corner_src, corners):
        packs = [zero, zero, zero, zero]
        for f, values in enumerate(fields):
            cols[0, f] = edge_rows(values, 0)
            cols[1, f] = edge_rows(values, SUB - 1)
            for side_x in range(2):
                for side_z in range(2):
                    at = 2 * side_x + side_z
                    x = MAIN - 1 if side_x == 0 else 0
                    z = SUB - 1 if side_z == 0 else 0
                    packs[at] = jnp.where(sub == f, full(values[x][z : z + 1, :]), packs[at])
        for at in range(4):
            corner_src[at] = packs[at]
        copies = halo_copies(ring, ext, cols, corner_src, corners)
        for goes, _, copy in copies:
            pl.when(goes)(copy.start)
        return copies

    def wait_halo(copies):
        for goes, comes, copy in copies:
            pl.when(goes)(copy.wait_send)
            pl.when(comes)(copy.wait_recv)

    def corner_rows(corners, f):
        result = zero
        for at in range(4):
            result = jnp.where(sub == at, full(corners[at][f : f + 1, :]), result)
        return result

    def shifted(values, low, high):
        before = jnp.where(sub == 0, full(low), pltpu.roll(values, 1, 0))
        after = jnp.where(sub == SUB - 1, full(high), pltpu.roll(values, SUB - 1, 0))
        return values + 0.5 * (before + after)

    def smear(v):
        planes = [v[XLO]] + [v[x] for x in range(MAIN)] + [v[XHI]]
        corner = v[CORNER]
        low = shifted(v[ZLO], corner[0:1, :], corner[2:3, :])
        high = shifted(v[ZHI], corner[1:2, :], corner[3:4, :])
        result = []
        for x in range(MAIN):
            mid = planes[x + 1] + 0.5 * (planes[x] + planes[x + 2])
            mid = shifted(mid, low[x : x + 1, :], high[x : x + 1, :])
            before = jnp.where(lane == 0, 0.0, pltpu.roll(mid, 1, 1))
            after = jnp.where(lane == LANES - 1, 0.0, pltpu.roll(mid, LANES - 1, 1))
            result.append(mid + 0.5 * (before + after))
        return result

    node = lax.broadcasted_iota(jnp.int32, (count, LANES), 0)
    node_lane = lax.broadcasted_iota(jnp.int32, (count, LANES), 1)
    member = lax.rem(node, members)

    def coarse_solve(source, inverse):
        guess = omega * source * inverse
        for sweep in range(SWEEPS - 1):
            beside = pltpu.roll(guess, 1, 1) + pltpu.roll(guess, LANES - 1, 1)
            beside = beside + jnp.where(member == 0, 0.0, pltpu.roll(guess, 1, 0))
            beside = beside + jnp.where(
                member == members - 1, 0.0, pltpu.roll(guess, count - 1, 0)
            )
            beside = beside + jnp.where(node < members, 0.0, pltpu.roll(guess, members, 0))
            beside = beside + jnp.where(
                node >= count - members, 0.0, pltpu.roll(guess, count - members, 0)
            )
            guess = (1.0 - omega) * guess + omega * (source + beside) * inverse
        return guess

    start = [r_ref[x] for x in range(MAIN)]
    first_row = restrict(start) + pltpu.roll(full(small[1, 0:1, :]), boxes, 1)

    def first_send(dot):
        pl.semaphore_wait(barrier, count - 1)
        send_rows(0, with_scalar(first_row, 0, dot))

    w = block_apply(start, first_send, True)
    for x in range(MAIN):
        first_ext[x, 0] = w[x]
    kappas = [first_ext[x, 1] for x in range(MAIN)]
    maps = [first_ext[x, 2] for x in range(MAIN)]
    copies = start_halo(
        0, [w, kappas, maps], first_ext, first_cols, first_corner_src, first_corners
    )
    gathered = wait_rows(0)
    diagonal = pltpu.roll(gathered, LANES - boxes, 1)
    inverse = jnp.where(
        node_lane < boxes, 1.0 / jnp.where(node_lane < boxes, 6.0 + diagonal, 1.0), 0.0
    )
    source = jnp.where(node_lane < boxes, gathered, 0.0)
    guess = coarse_solve(source, inverse)
    local_part = scalar(jnp.sum(gathered, axis=0, keepdims=True), 0)
    norm = local_part + total_of(source * guess) * (1.0 / restrict_scale)

    def guess_rows(guess):
        picks = {}
        for do in (-1, 0, 1):
            for dm in (-1, 0, 1):
                wanted = me + do * members + dm
                picks[(do, dm)] = full(
                    jnp.sum(jnp.where(node == wanted, guess, 0.0), axis=0, keepdims=True)
                )
        return picks

    def add_coarse(values, guess):
        picks = guess_rows(guess)
        result = []
        for x in range(MAIN):
            result.append(values[x] + take(picks[(0, 0)], amaps[x]))
        for slot, way in ((XLO, (-1, 0)), (XHI, (1, 0)), (ZLO, (0, -1)), (ZHI, (0, 1))):
            result.append(values[slot] + take(picks[way], amaps[slot]))
        corner = zero
        for at, way in enumerate(((-1, -1), (-1, 1), (1, -1), (1, 1))):
            corner = jnp.where(sub == at, take(picks[way], amaps[CORNER]), corner)
        result.append(values[CORNER] + corner)
        return result

    wait_halo(copies)
    for slot in range(SLOTS):
        if slot == CORNER:
            parts = [corner_rows(first_corners, f) for f in range(3)]
        else:
            parts = [first_ext[slot, f] for f in range(3)]
        w_ext[slot] = parts[0]
        kap[slot] = parts[1]
        if slot >= MAIN:
            amaps[slot] = (parts[2].astype(jnp.int32) + (LANES - 1)) & (LANES - 1)
    smeared = smear([kap[s] for s in range(SLOTS)])
    for x in range(MAIN):
        kt[x] = 8.0 * kap[x] + smeared[x]
        r_cur[x] = r_ref[x]
    z = add_coarse([w_ext[s] for s in range(SLOTS)], guess)
    for slot in range(SLOTS):
        p_ext[slot] = z[slot]

    for step in range(ITERS):
        last = step == ITERS - 1
        p = [p_ext[s] for s in range(SLOTS)]
        flat = smear(p)
        steep = smear([p[s] * kap[s] for s in range(SLOTS)])
        along, across = zero, zero
        for x in range(MAIN):
            q = p[x] * kt[x] - kap[x] * flat[x] - steep[x]
            q_cur[x] = q
            along = along + p[x] * q
            across = across + w_ext[x] * q
        image = [q_cur[x] for x in range(MAIN)]
        row = restrict(image)
        row = with_scalar(row, 0, total_of(along))
        row = with_scalar(row, 1, total_of(across))

        def later_send(dot, row=row, step=step):
            send_rows(1 + step, with_scalar(row, 2, dot))

        bq = block_apply(image, later_send)
        if not last:
            for x in range(MAIN):
                later_ext[x, 0] = bq[x]
            copies = start_halo(
                1 + step, [bq], later_ext, later_cols, later_corner_src, later_corners
            )
        gathered = wait_rows(1 + step)
        sums = jnp.sum(gathered, axis=0, keepdims=True)
        alpha = norm / scalar(sums, 0)
        source = source - alpha * jnp.where(node_lane < boxes, gathered, 0.0)
        guess = coarse_solve(source, inverse)
        local_part = (
            local_part - 2.0 * alpha * scalar(sums, 1) + alpha * alpha * scalar(sums, 2)
        )
        following = local_part + total_of(source * guess) * (1.0 / restrict_scale)
        beta = full(following / norm)
        alpha = full(alpha)
        norm = following
        for x in range(MAIN):
            moved_x = alpha * p_ext[x]
            x_out[x] = moved_x if step == 0 else x_out[x] + moved_x
            r_cur[x] = r_cur[x] - alpha * q_cur[x]
        if not last:
            wait_halo(copies)
            change = [later_ext[s, 0] for s in range(CORNER)] + [corner_rows(later_corners, 0)]
            for slot in range(SLOTS):
                w_ext[slot] = w_ext[slot] - alpha * change[slot]
            z = add_coarse([w_ext[s] for s in range(SLOTS)], guess)
            for slot in range(SLOTS):
                p_ext[slot] = z[slot] + beta * p_ext[slot]
        else:
            own = full(jnp.sum(jnp.where(node == me, guess, 0.0), axis=0, keepdims=True))
            for x in range(MAIN):
                z_x = w_ext[x] - alpha * bq[x] + take(own, amaps[x])
                p_out[x] = z_x + beta * p_ext[x]
                r_out[x] = r_cur[x]


def emit(x_ref, r_ref, p_ref, x_out, r_out, p_out, sems):
    pairs = ((x_ref, x_out), (r_ref, r_out), (p_ref, p_out))
    copies = [pltpu.make_async_copy(a, b, sems.at[i]) for i, (a, b) in enumerate(pairs)]
    for copy in copies:
        copy.start()
    for copy in copies:
        copy.wait()


def shards(
    owners, members, right_side, coefficient_index, material_coefficients, block_cells,
    block_inverses, aggregate_map, coarse_diagonal,
):
    blocks, side = block_cells.shape[2], block_cells.shape[3]
    assert right_side.shape == (SUB, SUB, LANES) and side == LANES and blocks == SUB * SUB
    count = owners * members
    groups = blocks // SUB
    field = jax.ShapeDtypeStruct(right_side.shape, jnp.float32)
    vmem = pl.BlockSpec(memory_space=pltpu.VMEM)
    f32, i32 = jnp.float32, jnp.int32
    tile = (SUB, LANES)
    hbm = pl.BlockSpec(memory_space=pltpu.HBM)
    results = pl.pallas_call(
        functools.partial(kernel, owners, members),
        out_shape=(field, field, field),
        in_specs=[hbm] * 7,
        out_specs=(vmem, vmem, vmem),
        scratch_shapes=[
            pltpu.VMEM(right_side.shape, f32),
            pltpu.VMEM(right_side.shape, i32),
            pltpu.VMEM((1,) + material_coefficients.shape, f32),
            pltpu.VMEM((groups,) + tile, i32),
            pltpu.VMEM(right_side.shape, i32),
            pltpu.VMEM(coarse_diagonal.shape, f32),
            pltpu.SemaphoreType.DMA((6,)),
            pltpu.VMEM((blocks, side, side), f32),
            pltpu.VMEM((blocks, side, 2 * side), jnp.bfloat16),
            pltpu.VMEM((blocks,) + tile, f32),
            pltpu.VMEM((groups,) + tile, i32),
            pltpu.VMEM((groups,) + tile, i32),
            pltpu.VMEM((groups,) + tile, i32),
            pltpu.VMEM((groups,) + tile, i32),
            pltpu.VMEM((groups,) + tile, f32),
            pltpu.VMEM((CORNER, 3) + tile, f32),
            pltpu.VMEM((2, 3) + tile, f32),
            pltpu.VMEM((4,) + tile, f32),
            pltpu.VMEM((4,) + tile, f32),
            pltpu.VMEM((CORNER, 1) + tile, f32),
            pltpu.VMEM((2, 1) + tile, f32),
            pltpu.VMEM((4,) + tile, f32),
            pltpu.VMEM((4,) + tile, f32),
            pltpu.VMEM((SLOTS,) + tile, f32),
            pltpu.VMEM((SLOTS,) + tile, i32),
            pltpu.VMEM((SLOTS,) + tile, f32),
            pltpu.VMEM((SLOTS,) + tile, f32),
            pltpu.VMEM((MAIN,) + tile, f32),
            pltpu.VMEM((MAIN,) + tile, f32),
            pltpu.VMEM((MAIN,) + tile, f32),
            pltpu.VMEM((2,) + tile, f32),
            pltpu.VMEM((1 + ITERS, 1, LANES), f32),
            pltpu.VMEM((1 + ITERS, count, 1, LANES), f32),
            pltpu.SemaphoreType.DMA((groups,)),
            pltpu.SemaphoreType.DMA((ITERS, len(DIRECTIONS))),
            pltpu.SemaphoreType.DMA((ITERS, len(DIRECTIONS))),
            pltpu.SemaphoreType.DMA((1 + ITERS,)),
            pltpu.SemaphoreType.DMA((1 + ITERS,)),
        ],
        compiler_params=pltpu.CompilerParams(
            collective_id=0, has_side_effects=True, vmem_limit_bytes=32 << 20
        ),
    )(
        *(pltpu.with_memory_space_constraint(a, pltpu.HBM) for a in (
        right_side,
        coefficient_index,
        material_coefficients.reshape(1, -1),
        block_cells.reshape(groups, SUB, LANES),
        block_inverses.reshape(blocks, side, side),
        aggregate_map,
        coarse_diagonal,
        ))
    )
    return pl.pallas_call(
        emit,
        out_shape=(field, field, field),
        in_specs=[vmem] * 3,
        out_specs=(hbm,) * 3,
        scratch_shapes=[pltpu.SemaphoreType.DMA((3,))],
        compiler_params=pltpu.CompilerParams(vmem_limit_bytes=1 << 20),
    )(*results)


def solution(mesh):
    three = P("coarse", "fine", None)
    return jax.shard_map(
        functools.partial(shards, mesh.shape["coarse"], mesh.shape["fine"]),
        mesh=mesh,
        in_specs=(
            three,
            three,
            P(),
            P("coarse", "fine", None, None),
            P("coarse", "fine", None, None, None),
            three,
            three,
        ),
        out_specs=(three, three, three),
        check_vma=False,
    )
```

```python
import functools

import jax
import jax.numpy as jnp
from jax import lax
from jax.experimental import pallas as pl
from jax.experimental.pallas import tpu as pltpu
from jax.sharding import PartitionSpec as P

ITERS = 2
SWEEPS = 4
omega = 0.8
restrict_scale = 0.25
MESH = pl.DeviceIdType.MESH
SUB = 8
LANES = 128
MAIN = 8
XLO, XHI, ZLO, ZHI, CORNER = 8, 9, 10, 11, 12
SLOTS = 13
DIRECTIONS = ((-1, 0), (1, 0), (0, -1), (0, 1), (-1, -1), (-1, 1), (1, -1), (1, 1))


def take(values, lanes):
    return jnp.take_along_axis(values, lanes, axis=1, mode="promise_in_bounds")


def full(row):
    return jnp.broadcast_to(row, (SUB, LANES))


def total_of(values):
    return jnp.sum(jnp.sum(values, axis=0, keepdims=True), axis=1, keepdims=True)


def kernel(
    owners, members, r_hbm, cidx_hbm, table_hbm, cells_hbm, inv_ref, amap_hbm, diag_hbm,
    x_out, r_out, p_out,
    r_ref, cidx_ref, table_ref, cells_ref, amap_ref, diag_ref, in_sems,
    mats, halves, rot, key_in, lane_in, key_out, lane_out, moved,
    first_ext, first_cols, first_corner_src, first_corners,
    later_ext, later_cols, later_corner_src, later_corners,
    kap, amaps, w_ext, p_ext, r_cur, q_cur, kt, small,
    row_src, rows,
    mat_sems, send_sems, recv_sems, row_send, row_recv,
):
    count = owners * members
    o = lax.axis_index("coarse")
    m = lax.axis_index("fine")
    me = o * members + m
    groups = cells_ref.shape[0]
    sub = lax.broadcasted_iota(jnp.int32, (SUB, LANES), 0)
    lane = lax.broadcasted_iota(jnp.int32, (SUB, LANES), 1)
    zero = jnp.zeros((SUB, LANES), jnp.float32)

    in_copies = [
        pltpu.make_async_copy(src, dst, in_sems.at[at])
        for at, (src, dst) in enumerate(
            (
                (cells_hbm, cells_ref),
                (r_hbm, r_ref),
                (amap_hbm, amap_ref),
                (cidx_hbm, cidx_ref),
                (table_hbm, table_ref),
                (diag_hbm, diag_ref),
            )
        )
    ]
    for copy in in_copies:
        copy.start()
    def mat_copy(u):
        part = pl.ds(u * SUB, SUB)
        return pltpu.make_async_copy(inv_ref.at[part], mats.at[part], mat_sems.at[u])

    for u in range(groups):
        mat_copy(u).start()

    for slot in range(MAIN, CORNER):
        for f in range(3):
            first_ext[slot, f] = zero
        later_ext[slot, 0] = zero
    for c in range(4):
        first_corners[c] = zero
        later_corners[c] = zero

    barrier = pltpu.get_barrier_semaphore()

    def other(d):
        t = lax.rem(me + d, count)
        return {"coarse": lax.div(t, members), "fine": lax.rem(t, members)}

    def announce(d, carry):
        pl.semaphore_signal(barrier, inc=1, device_id=other(d), device_id_type=MESH)
        return carry

    lax.fori_loop(1, count, announce, 0)

    in_copies[0].wait()

    def keys_of(source):
        row = lax.shift_right_logical(source, 7)
        turn = (jnp.bitwise_and(row, 7) - sub) & 7
        return jnp.bitwise_and(row, ~7) + turn, jnp.bitwise_and(source, 127)

    for g in range(groups):
        key, lanes = keys_of(cells_ref[g])
        key_in[g] = key
        lane_in[g] = lanes

    def load_turns(values):
        for g in range(len(values)):
            for turn in range(SUB):
                rot[g * SUB + turn] = (
                    values[g] if turn == 0 else pltpu.roll(values[g], SUB - turn, 0)
                )

    def permuted(key, lanes):
        parts = [zero, zero]
        for k in range(groups * SUB):
            parts[k % 2] = jnp.where(key == k, take(rot[k], lanes), parts[k % 2])
        return parts[0] + parts[1]

    tall = lax.broadcasted_iota(jnp.int32, (groups * SUB, LANES), 0)
    taller = lax.broadcasted_iota(jnp.int32, (LANES, LANES), 0)
    wide = lax.broadcasted_iota(jnp.int32, (groups * SUB, LANES), 1).astype(jnp.float32)

    def find(g, carry):
        block = cells_ref[g]
        for b in range(SUB):
            source = block[b : b + 1, :]
            hit = tall == jnp.broadcast_to(lax.shift_right_logical(source, 7), tall.shape)
            number = (g * SUB + b).astype(jnp.float32)
            left = jnp.concatenate(
                [jnp.where(hit, number, 0.0), jnp.where(hit, wide, 0.0)], axis=0
            ).astype(jnp.bfloat16)
            right = jnp.where(
                taller == jnp.broadcast_to(jnp.bitwise_and(source, 127), taller.shape), 1.0, 0.0
            ).astype(jnp.bfloat16)
            carry = carry + lax.dot_general(
                left, right, (((1,), (1,)), ((), ())), preferred_element_type=jnp.float32
            )
        return carry

    found = lax.fori_loop(
        0, groups, find, jnp.zeros((2 * groups * SUB, LANES), jnp.float32)
    ).astype(jnp.int32)
    for g in range(groups):
        block = found[g * SUB : (g + 1) * SUB]
        place = found[(groups + g) * SUB : (groups + g + 1) * SUB]
        key, lanes = keys_of(block * LANES + place)
        key_out[g] = key
        lane_out[g] = lanes

    for copy in in_copies[1:]:
        copy.wait()
    small[...] = jnp.zeros(small.shape, jnp.float32)
    small[0, 0:1, 0 : table_ref.shape[1]] = table_ref[...]
    small[1, 0:1, 0 : diag_ref.shape[2]] = diag_ref[0]
    boxes = diag_ref.shape[2]
    table = full(small[0, 0:1, :])
    for x in range(MAIN):
        first_ext[x, 1] = take(table, cidx_ref[x])
        first_ext[x, 2] = (amap_ref[x] + 1).astype(jnp.float32)
        amaps[x] = amap_ref[x]

    def split(values):
        high = values.astype(jnp.bfloat16)
        low = (values - high.astype(jnp.float32)).astype(jnp.bfloat16)
        return high, low

    def block_apply(values, done_with_dot, first=False):
        load_turns(values)

        def one(u, carry):
            dot, picked = carry
            if first:
                mat_copy(u).wait()
                for b in range(SUB):
                    high, low = split(mats[u * SUB + b])
                    halves[u * SUB + b, :, 0:LANES] = high
                    halves[u * SUB + b, :, LANES : 2 * LANES] = low
            ahead = lax.rem(u + 1, groups)
            upcoming = permuted(key_in[ahead], lane_in[ahead])
            left = jnp.concatenate(split(picked), axis=0)
            product = zero
            for b in range(SUB):
                both = jnp.dot(left, halves[u * SUB + b], preferred_element_type=jnp.float32)
                line = both[:SUB, :LANES] + (both[SUB:, :LANES] + both[:SUB, LANES:])
                line = line + both[SUB:, LANES:]
                product = jnp.where(sub == b, line, product)
            moved[u] = product
            return dot + picked * product, upcoming

        dot, _ = lax.fori_loop(0, groups, one, (zero, permuted(key_in[0], lane_in[0])))
        done_with_dot(total_of(dot))
        load_turns([moved[g] for g in range(groups)])

        def back(g, carry):
            for at in (2 * g, 2 * g + 1):
                moved[at] = permuted(key_out[at], lane_out[at])
            return carry

        lax.fori_loop(0, groups // 2, back, 0)
        return [moved[g] for g in range(groups)]

    base = lax.shift_right_logical(lane, 3)

    def restrict(values):
        sums = []
        for move in (-1, 0, 1):
            total = zero
            for x in range(MAIN):
                total = total + jnp.where(amaps[x] - base == move, values[x], 0.0)
            sums.append(total)
        total = pltpu.roll(sums[0], LANES - SUB, 1) + sums[1] + pltpu.roll(sums[2], SUB, 1)
        total = full(jnp.sum(total, axis=0, keepdims=True))
        for step in (1, 2, 4):
            total = total + pltpu.roll(total, LANES - step, 1)
        return jnp.where(lane < boxes, restrict_scale * take(total, (lane * SUB) & 127), 0.0)

    def row_copy(index, src, dst, device):
        return pltpu.make_async_remote_copy(
            src_ref=src, dst_ref=dst, send_sem=row_send.at[index], recv_sem=row_recv.at[index],
            device_id=device, device_id_type=MESH,
        )

    def send_rows(index, row):
        row_src[index] = row[0:1, :]
        rows[index, me] = row[0:1, :]

        def one(d, carry):
            row_copy(index, row_src.at[index], rows.at[index, me], other(d)).start()
            return carry

        lax.fori_loop(1, count, one, 0)

    def wait_rows(index):
        part = rows.at[index, pl.ds(0, count - 1)]
        both = row_copy(index, part, part, other(1))
        both.wait_send()
        both.wait_recv()
        return rows[index].reshape(count, LANES)

    def scalar(row, number):
        at = 2 * boxes + number
        return row[:, at : at + 1]

    def with_scalar(row, number, value):
        return jnp.where(lane == 2 * boxes + number, full(value), row)

    def edge_rows(values, z):
        result = zero
        for x in range(MAIN):
            result = jnp.where(sub == x, full(values[x][z : z + 1, :]), result)
        return result

    def halo_copies(ring, ext, cols, corner_src, corners):
        copies = []
        for number, (do, dm) in enumerate(DIRECTIONS):
            if dm == 0:
                src = ext.at[MAIN - 1 if do == 1 else 0]
                dst = ext.at[XLO if do == 1 else XHI]
            elif do == 0:
                src = cols.at[1 if dm == 1 else 0]
                dst = ext.at[ZLO if dm == 1 else ZHI]
            else:
                at = 2 * (0 if do == 1 else 1) + (0 if dm == 1 else 1)
                src = corner_src.at[at]
                dst = corners.at[at]
            to_o, to_m = o + do, m + dm
            from_o, from_m = o - do, m - dm
            goes = (to_o >= 0) & (to_o < owners) & (to_m >= 0) & (to_m < members)
            comes = (from_o >= 0) & (from_o < owners) & (from_m >= 0) & (from_m < members)
            copies.append(
                (
                    goes,
                    comes,
                    pltpu.make_async_remote_copy(
                        src_ref=src, dst_ref=dst,
                        send_sem=send_sems.at[ring, number], recv_sem=recv_sems.at[ring, number],
                        device_id={"coarse": to_o, "fine": to_m}, device_id_type=MESH,
                    ),
                )
            )
        return copies

    def start_halo(ring, fields, ext, cols, corner_src, corners):
        packs = [zero, zero, zero, zero]
        for f, values in enumerate(fields):
            cols[0, f] = edge_rows(values, 0)
            cols[1, f] = edge_rows(values, SUB - 1)
            for side_x in range(2):
                for side_z in range(2):
                    at = 2 * side_x + side_z
                    x = MAIN - 1 if side_x == 0 else 0
                    z = SUB - 1 if side_z == 0 else 0
                    packs[at] = jnp.where(sub == f, full(values[x][z : z + 1, :]), packs[at])
        for at in range(4):
            corner_src[at] = packs[at]
        copies = halo_copies(ring, ext, cols, corner_src, corners)
        for goes, _, copy in copies:
            pl.when(goes)(copy.start)
        return copies

    def wait_halo(copies):
        for goes, comes, copy in copies:
            pl.when(goes)(copy.wait_send)
            pl.when(comes)(copy.wait_recv)

    def corner_rows(corners, f):
        result = zero
        for at in range(4):
            result = jnp.where(sub == at, full(corners[at][f : f + 1, :]), result)
        return result

    def shifted(values, low, high):
        before = jnp.where(sub == 0, full(low), pltpu.roll(values, 1, 0))
        after = jnp.where(sub == SUB - 1, full(high), pltpu.roll(values, SUB - 1, 0))
        return values + 0.5 * (before + after)

    def smear(v):
        planes = [v[XLO]] + [v[x] for x in range(MAIN)] + [v[XHI]]
        corner = v[CORNER]
        low = shifted(v[ZLO], corner[0:1, :], corner[2:3, :])
        high = shifted(v[ZHI], corner[1:2, :], corner[3:4, :])
        result = []
        for x in range(MAIN):
            mid = planes[x + 1] + 0.5 * (planes[x] + planes[x + 2])
            mid = shifted(mid, low[x : x + 1, :], high[x : x + 1, :])
            before = jnp.where(lane == 0, 0.0, pltpu.roll(mid, 1, 1))
            after = jnp.where(lane == LANES - 1, 0.0, pltpu.roll(mid, LANES - 1, 1))
            result.append(mid + 0.5 * (before + after))
        return result

    node = lax.broadcasted_iota(jnp.int32, (count, LANES), 0)
    node_lane = lax.broadcasted_iota(jnp.int32, (count, LANES), 1)
    member = lax.rem(node, members)

    def coarse_solve(source, inverse):
        guess = omega * source * inverse
        for sweep in range(SWEEPS - 1):
            beside = pltpu.roll(guess, 1, 1) + pltpu.roll(guess, LANES - 1, 1)
            beside = beside + jnp.where(member == 0, 0.0, pltpu.roll(guess, 1, 0))
            beside = beside + jnp.where(
                member == members - 1, 0.0, pltpu.roll(guess, count - 1, 0)
            )
            beside = beside + jnp.where(node < members, 0.0, pltpu.roll(guess, members, 0))
            beside = beside + jnp.where(
                node >= count - members, 0.0, pltpu.roll(guess, count - members, 0)
            )
            guess = (1.0 - omega) * guess + omega * (source + beside) * inverse
        return guess

    start = [r_ref[x] for x in range(MAIN)]
    first_row = restrict(start) + pltpu.roll(full(small[1, 0:1, :]), boxes, 1)

    def first_send(dot):
        pl.semaphore_wait(barrier, count - 1)
        send_rows(0, with_scalar(first_row, 0, dot))

    w = block_apply(start, first_send, True)
    for x in range(MAIN):
        first_ext[x, 0] = w[x]
    kappas = [first_ext[x, 1] for x in range(MAIN)]
    maps = [first_ext[x, 2] for x in range(MAIN)]
    copies = start_halo(
        0, [w, kappas, maps], first_ext, first_cols, first_corner_src, first_corners
    )
    gathered = wait_rows(0)
    diagonal = pltpu.roll(gathered, LANES - boxes, 1)
    inverse = jnp.where(
        node_lane < boxes, 1.0 / jnp.where(node_lane < boxes, 6.0 + diagonal, 1.0), 0.0
    )
    source = jnp.where(node_lane < boxes, gathered, 0.0)
    guess = coarse_solve(source, inverse)
    local_part = scalar(jnp.sum(gathered, axis=0, keepdims=True), 0)
    norm = local_part + total_of(source * guess) * (1.0 / restrict_scale)

    def guess_rows(guess):
        picks = {}
        for do in (-1, 0, 1):
            for dm in (-1, 0, 1):
                wanted = me + do * members + dm
                picks[(do, dm)] = full(
                    jnp.sum(jnp.where(node == wanted, guess, 0.0), axis=0, keepdims=True)
                )
        return picks

    def add_coarse(values, guess):
        picks = guess_rows(guess)
        result = []
        for x in range(MAIN):
            result.append(values[x] + take(picks[(0, 0)], amaps[x]))
        for slot, way in ((XLO, (-1, 0)), (XHI, (1, 0)), (ZLO, (0, -1)), (ZHI, (0, 1))):
            result.append(values[slot] + take(picks[way], amaps[slot]))
        corner = zero
        for at, way in enumerate(((-1, -1), (-1, 1), (1, -1), (1, 1))):
            corner = jnp.where(sub == at, take(picks[way], amaps[CORNER]), corner)
        result.append(values[CORNER] + corner)
        return result

    wait_halo(copies)
    for slot in range(SLOTS):
        if slot == CORNER:
            parts = [corner_rows(first_corners, f) for f in range(3)]
        else:
            parts = [first_ext[slot, f] for f in range(3)]
        w_ext[slot] = parts[0]
        kap[slot] = parts[1]
        if slot >= MAIN:
            amaps[slot] = (parts[2].astype(jnp.int32) + (LANES - 1)) & (LANES - 1)
    smeared = smear([kap[s] for s in range(SLOTS)])
    for x in range(MAIN):
        kt[x] = 8.0 * kap[x] + smeared[x]
        r_cur[x] = r_ref[x]
    z = add_coarse([w_ext[s] for s in range(SLOTS)], guess)
    for slot in range(SLOTS):
        p_ext[slot] = z[slot]

    for step in range(ITERS):
        last = step == ITERS - 1
        p = [p_ext[s] for s in range(SLOTS)]
        flat = smear(p)
        steep = smear([p[s] * kap[s] for s in range(SLOTS)])
        along, across = zero, zero
        for x in range(MAIN):
            q = p[x] * kt[x] - kap[x] * flat[x] - steep[x]
            q_cur[x] = q
            along = along + p[x] * q
            across = across + w_ext[x] * q
        image = [q_cur[x] for x in range(MAIN)]
        row = restrict(image)
        row = with_scalar(row, 0, total_of(along))
        row = with_scalar(row, 1, total_of(across))

        def later_send(dot, row=row, step=step):
            send_rows(1 + step, with_scalar(row, 2, dot))

        bq = block_apply(image, later_send)
        if not last:
            for x in range(MAIN):
                later_ext[x, 0] = bq[x]
            copies = start_halo(
                1 + step, [bq], later_ext, later_cols, later_corner_src, later_corners
            )
        gathered = wait_rows(1 + step)
        sums = jnp.sum(gathered, axis=0, keepdims=True)
        alpha = norm / scalar(sums, 0)
        source = source - alpha * jnp.where(node_lane < boxes, gathered, 0.0)
        guess = coarse_solve(source, inverse)
        local_part = (
            local_part - 2.0 * alpha * scalar(sums, 1) + alpha * alpha * scalar(sums, 2)
        )
        following = local_part + total_of(source * guess) * (1.0 / restrict_scale)
        beta = full(following / norm)
        alpha = full(alpha)
        norm = following
        for x in range(MAIN):
            moved_x = alpha * p_ext[x]
            x_out[x] = moved_x if step == 0 else x_out[x] + moved_x
            r_cur[x] = r_cur[x] - alpha * q_cur[x]
        if not last:
            wait_halo(copies)
            change = [later_ext[s, 0] for s in range(CORNER)] + [corner_rows(later_corners, 0)]
            for slot in range(SLOTS):
                w_ext[slot] = w_ext[slot] - alpha * change[slot]
            z = add_coarse([w_ext[s] for s in range(SLOTS)], guess)
            for slot in range(SLOTS):
                p_ext[slot] = z[slot] + beta * p_ext[slot]
        else:
            own = full(jnp.sum(jnp.where(node == me, guess, 0.0), axis=0, keepdims=True))
            for x in range(MAIN):
                z_x = w_ext[x] - alpha * bq[x] + take(own, amaps[x])
                p_out[x] = z_x + beta * p_ext[x]
                r_out[x] = r_cur[x]


def emit(x_ref, r_ref, p_ref, x_out, r_out, p_out, sems):
    pairs = ((x_ref, x_out), (r_ref, r_out), (p_ref, p_out))
    copies = [pltpu.make_async_copy(a, b, sems.at[i]) for i, (a, b) in enumerate(pairs)]
    for copy in copies:
        copy.start()
    for copy in copies:
        copy.wait()


def shards(
    owners, members, right_side, coefficient_index, material_coefficients, block_cells,
    block_inverses, aggregate_map, coarse_diagonal,
):
    blocks, side = block_cells.shape[2], block_cells.shape[3]
    assert right_side.shape == (SUB, SUB, LANES) and side == LANES and blocks == SUB * SUB
    count = owners * members
    groups = blocks // SUB
    field = jax.ShapeDtypeStruct(right_side.shape, jnp.float32)
    vmem = pl.BlockSpec(memory_space=pltpu.VMEM)
    f32, i32 = jnp.float32, jnp.int32
    tile = (SUB, LANES)
    hbm = pl.BlockSpec(memory_space=pltpu.HBM)
    results = pl.pallas_call(
        functools.partial(kernel, owners, members),
        out_shape=(field, field, field),
        in_specs=[hbm] * 7,
        out_specs=(vmem, vmem, vmem),
        scratch_shapes=[
            pltpu.VMEM(right_side.shape, f32),
            pltpu.VMEM(right_side.shape, i32),
            pltpu.VMEM((1,) + material_coefficients.shape, f32),
            pltpu.VMEM((groups,) + tile, i32),
            pltpu.VMEM(right_side.shape, i32),
            pltpu.VMEM(coarse_diagonal.shape, f32),
            pltpu.SemaphoreType.DMA((6,)),
            pltpu.VMEM((blocks, side, side), f32),
            pltpu.VMEM((blocks, side, 2 * side), jnp.bfloat16),
            pltpu.VMEM((blocks,) + tile, f32),
            pltpu.VMEM((groups,) + tile, i32),
            pltpu.VMEM((groups,) + tile, i32),
            pltpu.VMEM((groups,) + tile, i32),
            pltpu.VMEM((groups,) + tile, i32),
            pltpu.VMEM((groups,) + tile, f32),
            pltpu.VMEM((CORNER, 3) + tile, f32),
            pltpu.VMEM((2, 3) + tile, f32),
            pltpu.VMEM((4,) + tile, f32),
            pltpu.VMEM((4,) + tile, f32),
            pltpu.VMEM((CORNER, 1) + tile, f32),
            pltpu.VMEM((2, 1) + tile, f32),
            pltpu.VMEM((4,) + tile, f32),
            pltpu.VMEM((4,) + tile, f32),
            pltpu.VMEM((SLOTS,) + tile, f32),
            pltpu.VMEM((SLOTS,) + tile, i32),
            pltpu.VMEM((SLOTS,) + tile, f32),
            pltpu.VMEM((SLOTS,) + tile, f32),
            pltpu.VMEM((MAIN,) + tile, f32),
            pltpu.VMEM((MAIN,) + tile, f32),
            pltpu.VMEM((MAIN,) + tile, f32),
            pltpu.VMEM((2,) + tile, f32),
            pltpu.VMEM((1 + ITERS, 1, LANES), f32),
            pltpu.VMEM((1 + ITERS, count, 1, LANES), f32),
            pltpu.SemaphoreType.DMA((groups,)),
            pltpu.SemaphoreType.DMA((ITERS, len(DIRECTIONS))),
            pltpu.SemaphoreType.DMA((ITERS, len(DIRECTIONS))),
            pltpu.SemaphoreType.DMA((1 + ITERS,)),
            pltpu.SemaphoreType.DMA((1 + ITERS,)),
        ],
        compiler_params=pltpu.CompilerParams(
            collective_id=0, has_side_effects=True, vmem_limit_bytes=32 << 20
        ),
    )(
        *(pltpu.with_memory_space_constraint(a, pltpu.HBM) for a in (
        right_side,
        coefficient_index,
        material_coefficients.reshape(1, -1),
        block_cells.reshape(groups, SUB, LANES),
        block_inverses.reshape(blocks, side, side),
        aggregate_map,
        coarse_diagonal,
        ))
    )
    return pl.pallas_call(
        emit,
        out_shape=(field, field, field),
        in_specs=[vmem] * 3,
        out_specs=(hbm,) * 3,
        scratch_shapes=[pltpu.SemaphoreType.DMA((3,))],
        compiler_params=pltpu.CompilerParams(vmem_limit_bytes=1 << 20),
    )(*results)


def solution(mesh):
    three = P("coarse", "fine", None)
    return jax.shard_map(
        functools.partial(shards, mesh.shape["coarse"], mesh.shape["fine"]),
        mesh=mesh,
        in_specs=(
            three,
            three,
            P(),
            P("coarse", "fine", None, None),
            P("coarse", "fine", None, None, None),
            three,
            three,
        ),
        out_specs=(three, three, three),
        check_vma=False,
    )
```

```python
import functools

import jax
import jax.numpy as jnp
from jax import lax
from jax.experimental import pallas as pl
from jax.experimental.pallas import tpu as pltpu
from jax.sharding import PartitionSpec as P

ITERS = 2
SWEEPS = 4
omega = 0.8
restrict_scale = 0.25
MESH = pl.DeviceIdType.MESH
SUB = 8
LANES = 128
MAIN = 8
XLO, XHI, ZLO, ZHI, CORNER = 8, 9, 10, 11, 12
SLOTS = 13
AHEAD = 4
DIRECTIONS = ((-1, 0), (1, 0), (0, -1), (0, 1), (-1, -1), (-1, 1), (1, -1), (1, 1))


def take(values, lanes):
    return jnp.take_along_axis(values, lanes, axis=1, mode="promise_in_bounds")


def full(row):
    return jnp.broadcast_to(row, (SUB, LANES))


def total_of(values):
    return jnp.sum(jnp.sum(values, axis=0, keepdims=True), axis=1, keepdims=True)


def kernel(
    owners, members, r_hbm, cidx_hbm, table_hbm, cells_hbm, inv_ref, amap_hbm, diag_hbm,
    x_out, r_out, p_out,
    r_ref, cidx_ref, table_ref, cells_ref, amap_ref, diag_ref, in_sems,
    mats, halves, rot, key_in, lane_in, key_out, lane_out, moved,
    first_ext, first_cols, first_corner_src, first_corners,
    later_ext, later_cols, later_corner_src, later_corners,
    kap, amaps, w_ext, p_ext, r_cur, q_cur, kt, small,
    row_src, rows,
    mat_sems, send_sems, recv_sems, row_send, row_recv,
):
    count = owners * members
    o = lax.axis_index("coarse")
    m = lax.axis_index("fine")
    me = o * members + m
    groups = cells_ref.shape[0]
    sub = lax.broadcasted_iota(jnp.int32, (SUB, LANES), 0)
    lane = lax.broadcasted_iota(jnp.int32, (SUB, LANES), 1)
    zero = jnp.zeros((SUB, LANES), jnp.float32)

    in_copies = [
        pltpu.make_async_copy(src, dst, in_sems.at[at])
        for at, (src, dst) in enumerate(
            (
                (cells_hbm, cells_ref),
                (r_hbm, r_ref),
                (amap_hbm, amap_ref),
                (cidx_hbm, cidx_ref),
                (table_hbm, table_ref),
                (diag_hbm, diag_ref),
            )
        )
    ]
    for copy in in_copies:
        copy.start()
    def mat_copy(u):
        part = pl.ds(u * SUB, SUB)
        return pltpu.make_async_copy(inv_ref.at[part], mats.at[part], mat_sems.at[u])

    for u in range(groups):
        mat_copy(u).start()

    for slot in range(MAIN, CORNER):
        for f in range(3):
            first_ext[slot, f] = zero
        later_ext[slot, 0] = zero
    for c in range(4):
        first_corners[c] = zero
        later_corners[c] = zero

    barrier = pltpu.get_barrier_semaphore()

    def other(d):
        t = lax.rem(me + d, count)
        return {"coarse": lax.div(t, members), "fine": lax.rem(t, members)}

    def announce(d, carry):
        pl.semaphore_signal(barrier, inc=1, device_id=other(d), device_id_type=MESH)
        return carry

    lax.fori_loop(1, count, announce, 0)

    in_copies[0].wait()

    def keys_of(source):
        row = lax.shift_right_logical(source, 7)
        turn = (jnp.bitwise_and(row, 7) - sub) & 7
        return jnp.bitwise_and(row, ~7) + turn, jnp.bitwise_and(source, 127)

    for g in range(groups):
        key, lanes = keys_of(cells_ref[g])
        key_in[g] = key
        lane_in[g] = lanes

    def load_turns(values):
        for g in range(len(values)):
            for turn in range(SUB):
                rot[g * SUB + turn] = (
                    values[g] if turn == 0 else pltpu.roll(values[g], SUB - turn, 0)
                )

    def permuted(key, lanes):
        parts = [zero, zero]
        for k in range(groups * SUB):
            parts[k % 2] = jnp.where(key == k, take(rot[k], lanes), parts[k % 2])
        return parts[0] + parts[1]

    tall = lax.broadcasted_iota(jnp.int32, (groups * SUB, LANES), 0)
    taller = lax.broadcasted_iota(jnp.int32, (LANES, LANES), 0)
    wide = lax.broadcasted_iota(jnp.int32, (groups * SUB, LANES), 1).astype(jnp.float32)

    def find(g, carry):
        block = cells_ref[g]
        for b in range(SUB):
            source = block[b : b + 1, :]
            hit = tall == jnp.broadcast_to(lax.shift_right_logical(source, 7), tall.shape)
            number = (g * SUB + b).astype(jnp.float32)
            left = jnp.concatenate(
                [jnp.where(hit, number, 0.0), jnp.where(hit, wide, 0.0)], axis=0
            ).astype(jnp.bfloat16)
            right = jnp.where(
                taller == jnp.broadcast_to(jnp.bitwise_and(source, 127), taller.shape), 1.0, 0.0
            ).astype(jnp.bfloat16)
            carry = carry + lax.dot_general(
                left, right, (((1,), (1,)), ((), ())), preferred_element_type=jnp.float32
            )
        return carry

    found = lax.fori_loop(
        0, groups, find, jnp.zeros((2 * groups * SUB, LANES), jnp.float32)
    ).astype(jnp.int32)
    for g in range(groups):
        block = found[g * SUB : (g + 1) * SUB]
        place = found[(groups + g) * SUB : (groups + g + 1) * SUB]
        key, lanes = keys_of(block * LANES + place)
        key_out[g] = key
        lane_out[g] = lanes

    for copy in in_copies[1:]:
        copy.wait()
    small[...] = jnp.zeros(small.shape, jnp.float32)
    small[0, 0:1, 0 : table_ref.shape[1]] = table_ref[...]
    small[1, 0:1, 0 : diag_ref.shape[2]] = diag_ref[0]
    boxes = diag_ref.shape[2]
    table = full(small[0, 0:1, :])
    for x in range(MAIN):
        first_ext[x, 1] = take(table, cidx_ref[x])
        first_ext[x, 2] = (amap_ref[x] + 1).astype(jnp.float32)
        amaps[x] = amap_ref[x]

    def split(values):
        high = values.astype(jnp.bfloat16)
        low = (values - high.astype(jnp.float32)).astype(jnp.bfloat16)
        return high, low

    def block_apply(values, done_with_dot, first=False):
        load_turns(values)

        def some(turn, carry):
            dot, picked = carry
            if first:
                for at in range(AHEAD):
                    mat_copy(turn * AHEAD + at).wait()
            for at in range(AHEAD):
                u = turn * AHEAD + at
                if first:
                    for b in range(SUB):
                        high, low = split(mats[u * SUB + b])
                        halves[u * SUB + b, :, 0:LANES] = high
                        halves[u * SUB + b, :, LANES : 2 * LANES] = low
                ahead = lax.rem(u + 1, groups)
                upcoming = permuted(key_in[ahead], lane_in[ahead])
                left = jnp.concatenate(split(picked), axis=0)
                product = zero
                for b in range(SUB):
                    both = jnp.dot(left, halves[u * SUB + b], preferred_element_type=jnp.float32)
                    line = both[:SUB, :LANES] + (both[SUB:, :LANES] + both[:SUB, LANES:])
                    line = line + both[SUB:, LANES:]
                    product = jnp.where(sub == b, line, product)
                moved[u] = product
                dot = dot + picked * product
                picked = upcoming
            return dot, picked

        dot, _ = lax.fori_loop(
            0, groups // AHEAD, some, (zero, permuted(key_in[0], lane_in[0]))
        )
        done_with_dot(total_of(dot))
        load_turns([moved[g] for g in range(groups)])

        def back(g, carry):
            for at in (4 * g, 4 * g + 1, 4 * g + 2, 4 * g + 3):
                moved[at] = permuted(key_out[at], lane_out[at])
            return carry

        lax.fori_loop(0, groups // 4, back, 0)
        return [moved[g] for g in range(groups)]

    base = lax.shift_right_logical(lane, 3)

    def restrict(values):
        sums = []
        for move in (-1, 0, 1):
            total = zero
            for x in range(MAIN):
                total = total + jnp.where(amaps[x] - base == move, values[x], 0.0)
            sums.append(total)
        total = pltpu.roll(sums[0], LANES - SUB, 1) + sums[1] + pltpu.roll(sums[2], SUB, 1)
        total = full(jnp.sum(total, axis=0, keepdims=True))
        for step in (1, 2, 4):
            total = total + pltpu.roll(total, LANES - step, 1)
        return jnp.where(lane < boxes, restrict_scale * take(total, (lane * SUB) & 127), 0.0)

    def row_copy(index, src, dst, device):
        return pltpu.make_async_remote_copy(
            src_ref=src, dst_ref=dst, send_sem=row_send.at[index], recv_sem=row_recv.at[index],
            device_id=device, device_id_type=MESH,
        )

    def send_rows(index, row):
        row_src[index] = row[0:1, :]
        rows[index, me] = row[0:1, :]

        def one(d, carry):
            row_copy(index, row_src.at[index], rows.at[index, me], other(d)).start()
            return carry

        lax.fori_loop(1, count, one, 0)

    def wait_rows(index):
        part = rows.at[index, pl.ds(0, count - 1)]
        both = row_copy(index, part, part, other(1))
        both.wait_send()
        both.wait_recv()
        return rows[index].reshape(count, LANES)

    def scalar(row, number):
        at = 2 * boxes + number
        return row[:, at : at + 1]

    def with_scalar(row, number, value):
        return jnp.where(lane == 2 * boxes + number, full(value), row)

    def edge_rows(values, z):
        result = zero
        for x in range(MAIN):
            result = jnp.where(sub == x, full(values[x][z : z + 1, :]), result)
        return result

    def halo_copies(ring, ext, cols, corner_src, corners):
        copies = []
        for number, (do, dm) in enumerate(DIRECTIONS):
            if dm == 0:
                src = ext.at[MAIN - 1 if do == 1 else 0]
                dst = ext.at[XLO if do == 1 else XHI]
            elif do == 0:
                src = cols.at[1 if dm == 1 else 0]
                dst = ext.at[ZLO if dm == 1 else ZHI]
            else:
                at = 2 * (0 if do == 1 else 1) + (0 if dm == 1 else 1)
                src = corner_src.at[at]
                dst = corners.at[at]
            to_o, to_m = o + do, m + dm
            from_o, from_m = o - do, m - dm
            goes = (to_o >= 0) & (to_o < owners) & (to_m >= 0) & (to_m < members)
            comes = (from_o >= 0) & (from_o < owners) & (from_m >= 0) & (from_m < members)
            copies.append(
                (
                    goes,
                    comes,
                    pltpu.make_async_remote_copy(
                        src_ref=src, dst_ref=dst,
                        send_sem=send_sems.at[ring, number], recv_sem=recv_sems.at[ring, number],
                        device_id={"coarse": to_o, "fine": to_m}, device_id_type=MESH,
                    ),
                )
            )
        return copies

    def start_halo(ring, fields, ext, cols, corner_src, corners):
        packs = [zero, zero, zero, zero]
        for f, values in enumerate(fields):
            cols[0, f] = edge_rows(values, 0)
            cols[1, f] = edge_rows(values, SUB - 1)
            for side_x in range(2):
                for side_z in range(2):
                    at = 2 * side_x + side_z
                    x = MAIN - 1 if side_x == 0 else 0
                    z = SUB - 1 if side_z == 0 else 0
                    packs[at] = jnp.where(sub == f, full(values[x][z : z + 1, :]), packs[at])
        for at in range(4):
            corner_src[at] = packs[at]
        copies = halo_copies(ring, ext, cols, corner_src, corners)
        for goes, _, copy in copies:
            pl.when(goes)(copy.start)
        return copies

    def wait_halo(copies):
        for goes, comes, copy in copies:
            pl.when(goes)(copy.wait_send)
            pl.when(comes)(copy.wait_recv)

    def corner_rows(corners, f):
        result = zero
        for at in range(4):
            result = jnp.where(sub == at, full(corners[at][f : f + 1, :]), result)
        return result

    def shifted(values, low, high):
        before = jnp.where(sub == 0, full(low), pltpu.roll(values, 1, 0))
        after = jnp.where(sub == SUB - 1, full(high), pltpu.roll(values, SUB - 1, 0))
        return values + 0.5 * (before + after)

    def smear(v):
        planes = [v[XLO]] + [v[x] for x in range(MAIN)] + [v[XHI]]
        corner = v[CORNER]
        low = shifted(v[ZLO], corner[0:1, :], corner[2:3, :])
        high = shifted(v[ZHI], corner[1:2, :], corner[3:4, :])
        result = []
        for x in range(MAIN):
            mid = planes[x + 1] + 0.5 * (planes[x] + planes[x + 2])
            mid = shifted(mid, low[x : x + 1, :], high[x : x + 1, :])
            before = jnp.where(lane == 0, 0.0, pltpu.roll(mid, 1, 1))
            after = jnp.where(lane == LANES - 1, 0.0, pltpu.roll(mid, LANES - 1, 1))
            result.append(mid + 0.5 * (before + after))
        return result

    node = lax.broadcasted_iota(jnp.int32, (count, LANES), 0)
    node_lane = lax.broadcasted_iota(jnp.int32, (count, LANES), 1)
    member = lax.rem(node, members)

    def coarse_solve(source, inverse):
        guess = omega * source * inverse
        for sweep in range(SWEEPS - 1):
            beside = pltpu.roll(guess, 1, 1) + pltpu.roll(guess, LANES - 1, 1)
            beside = beside + jnp.where(member == 0, 0.0, pltpu.roll(guess, 1, 0))
            beside = beside + jnp.where(
                member == members - 1, 0.0, pltpu.roll(guess, count - 1, 0)
            )
            beside = beside + jnp.where(node < members, 0.0, pltpu.roll(guess, members, 0))
            beside = beside + jnp.where(
                node >= count - members, 0.0, pltpu.roll(guess, count - members, 0)
            )
            guess = (1.0 - omega) * guess + omega * (source + beside) * inverse
        return guess

    start = [r_ref[x] for x in range(MAIN)]
    first_row = restrict(start) + pltpu.roll(full(small[1, 0:1, :]), boxes, 1)

    def first_send(dot):
        pl.semaphore_wait(barrier, count - 1)
        send_rows(0, with_scalar(first_row, 0, dot))

    w = block_apply(start, first_send, True)
    for x in range(MAIN):
        first_ext[x, 0] = w[x]
    kappas = [first_ext[x, 1] for x in range(MAIN)]
    maps = [first_ext[x, 2] for x in range(MAIN)]
    copies = start_halo(
        0, [w, kappas, maps], first_ext, first_cols, first_corner_src, first_corners
    )
    gathered = wait_rows(0)
    diagonal = pltpu.roll(gathered, LANES - boxes, 1)
    inverse = jnp.where(
        node_lane < boxes, 1.0 / jnp.where(node_lane < boxes, 6.0 + diagonal, 1.0), 0.0
    )
    source = jnp.where(node_lane < boxes, gathered, 0.0)
    guess = coarse_solve(source, inverse)
    local_part = scalar(jnp.sum(gathered, axis=0, keepdims=True), 0)
    norm = local_part + total_of(source * guess) * (1.0 / restrict_scale)

    def guess_rows(guess):
        picks = {}
        for do in (-1, 0, 1):
            for dm in (-1, 0, 1):
                wanted = me + do * members + dm
                picks[(do, dm)] = full(
                    jnp.sum(jnp.where(node == wanted, guess, 0.0), axis=0, keepdims=True)
                )
        return picks

    def add_coarse(values, guess):
        picks = guess_rows(guess)
        result = []
        for x in range(MAIN):
            result.append(values[x] + take(picks[(0, 0)], amaps[x]))
        for slot, way in ((XLO, (-1, 0)), (XHI, (1, 0)), (ZLO, (0, -1)), (ZHI, (0, 1))):
            result.append(values[slot] + take(picks[way], amaps[slot]))
        corner = zero
        for at, way in enumerate(((-1, -1), (-1, 1), (1, -1), (1, 1))):
            corner = jnp.where(sub == at, take(picks[way], amaps[CORNER]), corner)
        result.append(values[CORNER] + corner)
        return result

    wait_halo(copies)
    for slot in range(SLOTS):
        if slot == CORNER:
            parts = [corner_rows(first_corners, f) for f in range(3)]
        else:
            parts = [first_ext[slot, f] for f in range(3)]
        w_ext[slot] = parts[0]
        kap[slot] = parts[1]
        if slot >= MAIN:
            amaps[slot] = (parts[2].astype(jnp.int32) + (LANES - 1)) & (LANES - 1)
    smeared = smear([kap[s] for s in range(SLOTS)])
    for x in range(MAIN):
        kt[x] = 8.0 * kap[x] + smeared[x]
        r_cur[x] = r_ref[x]
    z = add_coarse([w_ext[s] for s in range(SLOTS)], guess)
    for slot in range(SLOTS):
        p_ext[slot] = z[slot]

    for step in range(ITERS):
        last = step == ITERS - 1
        p = [p_ext[s] for s in range(SLOTS)]
        flat = smear(p)
        steep = smear([p[s] * kap[s] for s in range(SLOTS)])
        along, across = zero, zero
        for x in range(MAIN):
            q = p[x] * kt[x] - kap[x] * flat[x] - steep[x]
            q_cur[x] = q
            along = along + p[x] * q
            across = across + w_ext[x] * q
        image = [q_cur[x] for x in range(MAIN)]
        row = restrict(image)
        row = with_scalar(row, 0, total_of(along))
        row = with_scalar(row, 1, total_of(across))

        def later_send(dot, row=row, step=step):
            send_rows(1 + step, with_scalar(row, 2, dot))

        bq = block_apply(image, later_send)
        if not last:
            for x in range(MAIN):
                later_ext[x, 0] = bq[x]
            copies = start_halo(
                1 + step, [bq], later_ext, later_cols, later_corner_src, later_corners
            )
        gathered = wait_rows(1 + step)
        sums = jnp.sum(gathered, axis=0, keepdims=True)
        alpha = norm / scalar(sums, 0)
        source = source - alpha * jnp.where(node_lane < boxes, gathered, 0.0)
        guess = coarse_solve(source, inverse)
        local_part = (
            local_part - 2.0 * alpha * scalar(sums, 1) + alpha * alpha * scalar(sums, 2)
        )
        following = local_part + total_of(source * guess) * (1.0 / restrict_scale)
        beta = full(following / norm)
        alpha = full(alpha)
        norm = following
        for x in range(MAIN):
            moved_x = alpha * p_ext[x]
            x_out[x] = moved_x if step == 0 else x_out[x] + moved_x
            r_cur[x] = r_cur[x] - alpha * q_cur[x]
        if not last:
            wait_halo(copies)
            change = [later_ext[s, 0] for s in range(CORNER)] + [corner_rows(later_corners, 0)]
            for slot in range(SLOTS):
                w_ext[slot] = w_ext[slot] - alpha * change[slot]
            z = add_coarse([w_ext[s] for s in range(SLOTS)], guess)
            for slot in range(SLOTS):
                p_ext[slot] = z[slot] + beta * p_ext[slot]
        else:
            own = full(jnp.sum(jnp.where(node == me, guess, 0.0), axis=0, keepdims=True))
            for x in range(MAIN):
                z_x = w_ext[x] - alpha * bq[x] + take(own, amaps[x])
                p_out[x] = z_x + beta * p_ext[x]
                r_out[x] = r_cur[x]


def emit(x_ref, r_ref, p_ref, x_out, r_out, p_out, sems):
    pairs = ((x_ref, x_out), (r_ref, r_out), (p_ref, p_out))
    copies = [pltpu.make_async_copy(a, b, sems.at[i]) for i, (a, b) in enumerate(pairs)]
    for copy in copies:
        copy.start()
    for copy in copies:
        copy.wait()


def shards(
    owners, members, right_side, coefficient_index, material_coefficients, block_cells,
    block_inverses, aggregate_map, coarse_diagonal,
):
    blocks, side = block_cells.shape[2], block_cells.shape[3]
    assert right_side.shape == (SUB, SUB, LANES) and side == LANES and blocks == SUB * SUB
    count = owners * members
    groups = blocks // SUB
    field = jax.ShapeDtypeStruct(right_side.shape, jnp.float32)
    vmem = pl.BlockSpec(memory_space=pltpu.VMEM)
    f32, i32 = jnp.float32, jnp.int32
    tile = (SUB, LANES)
    hbm = pl.BlockSpec(memory_space=pltpu.HBM)
    results = pl.pallas_call(
        functools.partial(kernel, owners, members),
        out_shape=(field, field, field),
        in_specs=[hbm] * 7,
        out_specs=(vmem, vmem, vmem),
        scratch_shapes=[
            pltpu.VMEM(right_side.shape, f32),
            pltpu.VMEM(right_side.shape, i32),
            pltpu.VMEM((1,) + material_coefficients.shape, f32),
            pltpu.VMEM((groups,) + tile, i32),
            pltpu.VMEM(right_side.shape, i32),
            pltpu.VMEM(coarse_diagonal.shape, f32),
            pltpu.SemaphoreType.DMA((6,)),
            pltpu.VMEM((blocks, side, side), f32),
            pltpu.VMEM((blocks, side, 2 * side), jnp.bfloat16),
            pltpu.VMEM((blocks,) + tile, f32),
            pltpu.VMEM((groups,) + tile, i32),
            pltpu.VMEM((groups,) + tile, i32),
            pltpu.VMEM((groups,) + tile, i32),
            pltpu.VMEM((groups,) + tile, i32),
            pltpu.VMEM((groups,) + tile, f32),
            pltpu.VMEM((CORNER, 3) + tile, f32),
            pltpu.VMEM((2, 3) + tile, f32),
            pltpu.VMEM((4,) + tile, f32),
            pltpu.VMEM((4,) + tile, f32),
            pltpu.VMEM((CORNER, 1) + tile, f32),
            pltpu.VMEM((2, 1) + tile, f32),
            pltpu.VMEM((4,) + tile, f32),
            pltpu.VMEM((4,) + tile, f32),
            pltpu.VMEM((SLOTS,) + tile, f32),
            pltpu.VMEM((SLOTS,) + tile, i32),
            pltpu.VMEM((SLOTS,) + tile, f32),
            pltpu.VMEM((SLOTS,) + tile, f32),
            pltpu.VMEM((MAIN,) + tile, f32),
            pltpu.VMEM((MAIN,) + tile, f32),
            pltpu.VMEM((MAIN,) + tile, f32),
            pltpu.VMEM((2,) + tile, f32),
            pltpu.VMEM((1 + ITERS, 1, LANES), f32),
            pltpu.VMEM((1 + ITERS, count, 1, LANES), f32),
            pltpu.SemaphoreType.DMA((groups,)),
            pltpu.SemaphoreType.DMA((ITERS, len(DIRECTIONS))),
            pltpu.SemaphoreType.DMA((ITERS, len(DIRECTIONS))),
            pltpu.SemaphoreType.DMA((1 + ITERS,)),
            pltpu.SemaphoreType.DMA((1 + ITERS,)),
        ],
        compiler_params=pltpu.CompilerParams(
            collective_id=0, has_side_effects=True, vmem_limit_bytes=32 << 20
        ),
    )(
        *(pltpu.with_memory_space_constraint(a, pltpu.HBM) for a in (
        right_side,
        coefficient_index,
        material_coefficients.reshape(1, -1),
        block_cells.reshape(groups, SUB, LANES),
        block_inverses.reshape(blocks, side, side),
        aggregate_map,
        coarse_diagonal,
        ))
    )
    return pl.pallas_call(
        emit,
        out_shape=(field, field, field),
        in_specs=[vmem] * 3,
        out_specs=(hbm,) * 3,
        scratch_shapes=[pltpu.SemaphoreType.DMA((3,))],
        compiler_params=pltpu.CompilerParams(vmem_limit_bytes=1 << 20),
    )(*results)


def solution(mesh):
    three = P("coarse", "fine", None)
    return jax.shard_map(
        functools.partial(shards, mesh.shape["coarse"], mesh.shape["fine"]),
        mesh=mesh,
        in_specs=(
            three,
            three,
            P(),
            P("coarse", "fine", None, None),
            P("coarse", "fine", None, None, None),
            three,
            three,
        ),
        out_specs=(three, three, three),
        check_vma=False,
    )
```

```python
import functools

import jax
import jax.numpy as jnp
from jax import lax
from jax.experimental import pallas as pl
from jax.experimental.pallas import tpu as pltpu
from jax.sharding import PartitionSpec as P

ITERS = 2
SWEEPS = 4
omega = 0.8
restrict_scale = 0.25
MESH = pl.DeviceIdType.MESH
SUB = 8
LANES = 128
MAIN = 8
XLO, XHI, ZLO, ZHI, CORNER = 8, 9, 10, 11, 12
SLOTS = 13
AHEAD = 8
DIRECTIONS = ((-1, 0), (1, 0), (0, -1), (0, 1), (-1, -1), (-1, 1), (1, -1), (1, 1))


def take(values, lanes):
    return jnp.take_along_axis(values, lanes, axis=1, mode="promise_in_bounds")


def full(row):
    return jnp.broadcast_to(row, (SUB, LANES))


def total_of(values):
    return jnp.sum(jnp.sum(values, axis=0, keepdims=True), axis=1, keepdims=True)


def kernel(
    owners, members, r_hbm, cidx_hbm, table_hbm, cells_hbm, inv_ref, amap_hbm, diag_hbm,
    x_out, r_out, p_out,
    r_ref, cidx_ref, table_ref, cells_ref, amap_ref, diag_ref, in_sems,
    mats, halves, rot, key_in, lane_in, key_out, lane_out, moved,
    first_ext, first_cols, first_corner_src, first_corners,
    later_ext, later_cols, later_corner_src, later_corners,
    kap, amaps, w_ext, p_ext, r_cur, q_cur, kt, small,
    row_src, rows,
    mat_sems, send_sems, recv_sems, row_send, row_recv,
):
    count = owners * members
    o = lax.axis_index("coarse")
    m = lax.axis_index("fine")
    me = o * members + m
    groups = cells_ref.shape[0]
    sub = lax.broadcasted_iota(jnp.int32, (SUB, LANES), 0)
    lane = lax.broadcasted_iota(jnp.int32, (SUB, LANES), 1)
    zero = jnp.zeros((SUB, LANES), jnp.float32)

    in_copies = [
        pltpu.make_async_copy(src, dst, in_sems.at[at])
        for at, (src, dst) in enumerate(
            (
                (cells_hbm, cells_ref),
                (r_hbm, r_ref),
                (amap_hbm, amap_ref),
                (cidx_hbm, cidx_ref),
                (table_hbm, table_ref),
                (diag_hbm, diag_ref),
            )
        )
    ]
    for copy in in_copies:
        copy.start()
    def mat_copy(u):
        part = pl.ds(u * SUB, SUB)
        return pltpu.make_async_copy(inv_ref.at[part], mats.at[part], mat_sems.at[u])

    for u in range(groups):
        mat_copy(u).start()

    for slot in range(MAIN, CORNER):
        for f in range(3):
            first_ext[slot, f] = zero
        later_ext[slot, 0] = zero
    for c in range(4):
        first_corners[c] = zero
        later_corners[c] = zero

    barrier = pltpu.get_barrier_semaphore()

    def other(d):
        t = lax.rem(me + d, count)
        return {"coarse": lax.div(t, members), "fine": lax.rem(t, members)}

    def announce(d, carry):
        pl.semaphore_signal(barrier, inc=1, device_id=other(d), device_id_type=MESH)
        return carry

    lax.fori_loop(1, count, announce, 0)

    in_copies[0].wait()

    def keys_of(source):
        row = lax.shift_right_logical(source, 7)
        turn = (jnp.bitwise_and(row, 7) - sub) & 7
        return jnp.bitwise_and(row, ~7) + turn, jnp.bitwise_and(source, 127)

    for g in range(groups):
        key, lanes = keys_of(cells_ref[g])
        key_in[g] = key
        lane_in[g] = lanes

    def load_turns(values):
        for g in range(len(values)):
            for turn in range(SUB):
                rot[g * SUB + turn] = (
                    values[g] if turn == 0 else pltpu.roll(values[g], SUB - turn, 0)
                )

    def permuted(key, lanes):
        parts = [zero, zero]
        for k in range(groups * SUB):
            parts[k % 2] = jnp.where(key == k, take(rot[k], lanes), parts[k % 2])
        return parts[0] + parts[1]

    tall = lax.broadcasted_iota(jnp.int32, (groups * SUB, LANES), 0)
    taller = lax.broadcasted_iota(jnp.int32, (LANES, LANES), 0)
    wide = lax.broadcasted_iota(jnp.int32, (groups * SUB, LANES), 1).astype(jnp.float32)

    def find_one(g, carry):
        block = cells_ref[g]
        for b in range(SUB):
            source = block[b : b + 1, :]
            hit = tall == jnp.broadcast_to(lax.shift_right_logical(source, 7), tall.shape)
            number = (g * SUB + b).astype(jnp.float32)
            left = jnp.concatenate(
                [jnp.where(hit, number, 0.0), jnp.where(hit, wide, 0.0)], axis=0
            ).astype(jnp.bfloat16)
            right = jnp.where(
                taller == jnp.broadcast_to(jnp.bitwise_and(source, 127), taller.shape), 1.0, 0.0
            ).astype(jnp.bfloat16)
            carry = carry + lax.dot_general(
                left, right, (((1,), (1,)), ((), ())), preferred_element_type=jnp.float32
            )
        return carry

    def find(turn, carry):
        return find_one(2 * turn + 1, find_one(2 * turn, carry))

    found = lax.fori_loop(
        0, groups // 2, find, jnp.zeros((2 * groups * SUB, LANES), jnp.float32)
    ).astype(jnp.int32)
    for g in range(groups):
        block = found[g * SUB : (g + 1) * SUB]
        place = found[(groups + g) * SUB : (groups + g + 1) * SUB]
        key, lanes = keys_of(block * LANES + place)
        key_out[g] = key
        lane_out[g] = lanes

    for copy in in_copies[1:]:
        copy.wait()
    small[...] = jnp.zeros(small.shape, jnp.float32)
    small[0, 0:1, 0 : table_ref.shape[1]] = table_ref[...]
    small[1, 0:1, 0 : diag_ref.shape[2]] = diag_ref[0]
    boxes = diag_ref.shape[2]
    table = full(small[0, 0:1, :])
    for x in range(MAIN):
        first_ext[x, 1] = take(table, cidx_ref[x])
        first_ext[x, 2] = (amap_ref[x] + 1).astype(jnp.float32)
        amaps[x] = amap_ref[x]

    def split(values):
        high = values.astype(jnp.bfloat16)
        low = (values - high.astype(jnp.float32)).astype(jnp.bfloat16)
        return high, low

    def block_apply(values, done_with_dot, first=False):
        load_turns(values)

        def some(turn, carry):
            dot, picked = carry
            if first:
                for at in range(AHEAD):
                    mat_copy(turn * AHEAD + at).wait()
            for at in range(AHEAD):
                u = turn * AHEAD + at
                if first:
                    for b in range(SUB):
                        high, low = split(mats[u * SUB + b])
                        halves[u * SUB + b, :, 0:LANES] = high
                        halves[u * SUB + b, :, LANES : 2 * LANES] = low
                ahead = lax.rem(u + 1, groups)
                upcoming = permuted(key_in[ahead], lane_in[ahead])
                left = jnp.concatenate(split(picked), axis=0)
                product = zero
                for b in range(SUB):
                    both = jnp.dot(left, halves[u * SUB + b], preferred_element_type=jnp.float32)
                    line = both[:SUB, :LANES] + (both[SUB:, :LANES] + both[:SUB, LANES:])
                    line = line + both[SUB:, LANES:]
                    product = jnp.where(sub == b, line, product)
                moved[u] = product
                dot = dot + picked * product
                picked = upcoming
            return dot, picked

        dot, _ = lax.fori_loop(
            0, groups // AHEAD, some, (zero, permuted(key_in[0], lane_in[0]))
        )
        done_with_dot(total_of(dot))
        load_turns([moved[g] for g in range(groups)])

        def back(g, carry):
            for step in range(AHEAD):
                at = g * AHEAD + step
                moved[at] = permuted(key_out[at], lane_out[at])
            return carry

        lax.fori_loop(0, groups // AHEAD, back, 0)
        return [moved[g] for g in range(groups)]

    base = lax.shift_right_logical(lane, 3)

    def restrict(values):
        sums = []
        for move in (-1, 0, 1):
            total = zero
            for x in range(MAIN):
                total = total + jnp.where(amaps[x] - base == move, values[x], 0.0)
            sums.append(total)
        total = pltpu.roll(sums[0], LANES - SUB, 1) + sums[1] + pltpu.roll(sums[2], SUB, 1)
        total = full(jnp.sum(total, axis=0, keepdims=True))
        for step in (1, 2, 4):
            total = total + pltpu.roll(total, LANES - step, 1)
        return jnp.where(lane < boxes, restrict_scale * take(total, (lane * SUB) & 127), 0.0)

    def row_copy(index, src, dst, device):
        return pltpu.make_async_remote_copy(
            src_ref=src, dst_ref=dst, send_sem=row_send.at[index], recv_sem=row_recv.at[index],
            device_id=device, device_id_type=MESH,
        )

    def send_rows(index, row):
        row_src[index] = row[0:1, :]
        rows[index, me] = row[0:1, :]

        def one(d, carry):
            row_copy(index, row_src.at[index], rows.at[index, me], other(d)).start()
            return carry

        lax.fori_loop(1, count, one, 0)

    def wait_rows(index):
        part = rows.at[index, pl.ds(0, count - 1)]
        both = row_copy(index, part, part, other(1))
        both.wait_send()
        both.wait_recv()
        return rows[index].reshape(count, LANES)

    def scalar(row, number):
        at = 2 * boxes + number
        return row[:, at : at + 1]

    def with_scalar(row, number, value):
        return jnp.where(lane == 2 * boxes + number, full(value), row)

    def edge_rows(values, z):
        result = zero
        for x in range(MAIN):
            result = jnp.where(sub == x, full(values[x][z : z + 1, :]), result)
        return result

    def halo_copies(ring, ext, cols, corner_src, corners):
        copies = []
        for number, (do, dm) in enumerate(DIRECTIONS):
            if dm == 0:
                src = ext.at[MAIN - 1 if do == 1 else 0]
                dst = ext.at[XLO if do == 1 else XHI]
            elif do == 0:
                src = cols.at[1 if dm == 1 else 0]
                dst = ext.at[ZLO if dm == 1 else ZHI]
            else:
                at = 2 * (0 if do == 1 else 1) + (0 if dm == 1 else 1)
                src = corner_src.at[at]
                dst = corners.at[at]
            to_o, to_m = o + do, m + dm
            from_o, from_m = o - do, m - dm
            goes = (to_o >= 0) & (to_o < owners) & (to_m >= 0) & (to_m < members)
            comes = (from_o >= 0) & (from_o < owners) & (from_m >= 0) & (from_m < members)
            copies.append(
                (
                    goes,
                    comes,
                    pltpu.make_async_remote_copy(
                        src_ref=src, dst_ref=dst,
                        send_sem=send_sems.at[ring, number], recv_sem=recv_sems.at[ring, number],
                        device_id={"coarse": to_o, "fine": to_m}, device_id_type=MESH,
                    ),
                )
            )
        return copies

    def start_halo(ring, fields, ext, cols, corner_src, corners):
        packs = [zero, zero, zero, zero]
        for f, values in enumerate(fields):
            cols[0, f] = edge_rows(values, 0)
            cols[1, f] = edge_rows(values, SUB - 1)
            for side_x in range(2):
                for side_z in range(2):
                    at = 2 * side_x + side_z
                    x = MAIN - 1 if side_x == 0 else 0
                    z = SUB - 1 if side_z == 0 else 0
                    packs[at] = jnp.where(sub == f, full(values[x][z : z + 1, :]), packs[at])
        for at in range(4):
            corner_src[at] = packs[at]
        copies = halo_copies(ring, ext, cols, corner_src, corners)
        for goes, _, copy in copies:
            pl.when(goes)(copy.start)
        return copies

    def wait_halo(copies):
        for goes, comes, copy in copies:
            pl.when(goes)(copy.wait_send)
            pl.when(comes)(copy.wait_recv)

    def corner_rows(corners, f):
        result = zero
        for at in range(4):
            result = jnp.where(sub == at, full(corners[at][f : f + 1, :]), result)
        return result

    def shifted(values, low, high):
        before = jnp.where(sub == 0, full(low), pltpu.roll(values, 1, 0))
        after = jnp.where(sub == SUB - 1, full(high), pltpu.roll(values, SUB - 1, 0))
        return values + 0.5 * (before + after)

    def smear(v):
        planes = [v[XLO]] + [v[x] for x in range(MAIN)] + [v[XHI]]
        corner = v[CORNER]
        low = shifted(v[ZLO], corner[0:1, :], corner[2:3, :])
        high = shifted(v[ZHI], corner[1:2, :], corner[3:4, :])
        result = []
        for x in range(MAIN):
            mid = planes[x + 1] + 0.5 * (planes[x] + planes[x + 2])
            mid = shifted(mid, low[x : x + 1, :], high[x : x + 1, :])
            before = jnp.where(lane == 0, 0.0, pltpu.roll(mid, 1, 1))
            after = jnp.where(lane == LANES - 1, 0.0, pltpu.roll(mid, LANES - 1, 1))
            result.append(mid + 0.5 * (before + after))
        return result

    node = lax.broadcasted_iota(jnp.int32, (count, LANES), 0)
    node_lane = lax.broadcasted_iota(jnp.int32, (count, LANES), 1)
    member = lax.rem(node, members)

    def coarse_solve(source, inverse):
        guess = omega * source * inverse
        for sweep in range(SWEEPS - 1):
            beside = pltpu.roll(guess, 1, 1) + pltpu.roll(guess, LANES - 1, 1)
            beside = beside + jnp.where(member == 0, 0.0, pltpu.roll(guess, 1, 0))
            beside = beside + jnp.where(
                member == members - 1, 0.0, pltpu.roll(guess, count - 1, 0)
            )
            beside = beside + jnp.where(node < members, 0.0, pltpu.roll(guess, members, 0))
            beside = beside + jnp.where(
                node >= count - members, 0.0, pltpu.roll(guess, count - members, 0)
            )
            guess = (1.0 - omega) * guess + omega * (source + beside) * inverse
        return guess

    start = [r_ref[x] for x in range(MAIN)]
    first_row = restrict(start) + pltpu.roll(full(small[1, 0:1, :]), boxes, 1)

    def first_send(dot):
        pl.semaphore_wait(barrier, count - 1)
        send_rows(0, with_scalar(first_row, 0, dot))

    w = block_apply(start, first_send, True)
    for x in range(MAIN):
        first_ext[x, 0] = w[x]
    kappas = [first_ext[x, 1] for x in range(MAIN)]
    maps = [first_ext[x, 2] for x in range(MAIN)]
    copies = start_halo(
        0, [w, kappas, maps], first_ext, first_cols, first_corner_src, first_corners
    )
    gathered = wait_rows(0)
    diagonal = pltpu.roll(gathered, LANES - boxes, 1)
    inverse = jnp.where(
        node_lane < boxes, 1.0 / jnp.where(node_lane < boxes, 6.0 + diagonal, 1.0), 0.0
    )
    source = jnp.where(node_lane < boxes, gathered, 0.0)
    guess = coarse_solve(source, inverse)
    local_part = scalar(jnp.sum(gathered, axis=0, keepdims=True), 0)
    norm = local_part + total_of(source * guess) * (1.0 / restrict_scale)

    def guess_rows(guess):
        picks = {}
        for do in (-1, 0, 1):
            for dm in (-1, 0, 1):
                wanted = me + do * members + dm
                picks[(do, dm)] = full(
                    jnp.sum(jnp.where(node == wanted, guess, 0.0), axis=0, keepdims=True)
                )
        return picks

    def add_coarse(values, guess):
        picks = guess_rows(guess)
        result = []
        for x in range(MAIN):
            result.append(values[x] + take(picks[(0, 0)], amaps[x]))
        for slot, way in ((XLO, (-1, 0)), (XHI, (1, 0)), (ZLO, (0, -1)), (ZHI, (0, 1))):
            result.append(values[slot] + take(picks[way], amaps[slot]))
        corner = zero
        for at, way in enumerate(((-1, -1), (-1, 1), (1, -1), (1, 1))):
            corner = jnp.where(sub == at, take(picks[way], amaps[CORNER]), corner)
        result.append(values[CORNER] + corner)
        return result

    wait_halo(copies)
    for slot in range(SLOTS):
        if slot == CORNER:
            parts = [corner_rows(first_corners, f) for f in range(3)]
        else:
            parts = [first_ext[slot, f] for f in range(3)]
        w_ext[slot] = parts[0]
        kap[slot] = parts[1]
        if slot >= MAIN:
            amaps[slot] = (parts[2].astype(jnp.int32) + (LANES - 1)) & (LANES - 1)
    smeared = smear([kap[s] for s in range(SLOTS)])
    for x in range(MAIN):
        kt[x] = 8.0 * kap[x] + smeared[x]
        r_cur[x] = r_ref[x]
    z = add_coarse([w_ext[s] for s in range(SLOTS)], guess)
    for slot in range(SLOTS):
        p_ext[slot] = z[slot]

    for step in range(ITERS):
        last = step == ITERS - 1
        p = [p_ext[s] for s in range(SLOTS)]
        flat = smear(p)
        steep = smear([p[s] * kap[s] for s in range(SLOTS)])
        along, across = zero, zero
        for x in range(MAIN):
            q = p[x] * kt[x] - kap[x] * flat[x] - steep[x]
            q_cur[x] = q
            along = along + p[x] * q
            across = across + w_ext[x] * q
        image = [q_cur[x] for x in range(MAIN)]
        row = restrict(image)
        row = with_scalar(row, 0, total_of(along))
        row = with_scalar(row, 1, total_of(across))

        def later_send(dot, row=row, step=step):
            send_rows(1 + step, with_scalar(row, 2, dot))

        bq = block_apply(image, later_send)
        if not last:
            for x in range(MAIN):
                later_ext[x, 0] = bq[x]
            copies = start_halo(
                1 + step, [bq], later_ext, later_cols, later_corner_src, later_corners
            )
        gathered = wait_rows(1 + step)
        sums = jnp.sum(gathered, axis=0, keepdims=True)
        alpha = norm / scalar(sums, 0)
        source = source - alpha * jnp.where(node_lane < boxes, gathered, 0.0)
        guess = coarse_solve(source, inverse)
        local_part = (
            local_part - 2.0 * alpha * scalar(sums, 1) + alpha * alpha * scalar(sums, 2)
        )
        following = local_part + total_of(source * guess) * (1.0 / restrict_scale)
        beta = full(following / norm)
        alpha = full(alpha)
        norm = following
        for x in range(MAIN):
            moved_x = alpha * p_ext[x]
            x_out[x] = moved_x if step == 0 else x_out[x] + moved_x
            r_cur[x] = r_cur[x] - alpha * q_cur[x]
        if not last:
            wait_halo(copies)
            change = [later_ext[s, 0] for s in range(CORNER)] + [corner_rows(later_corners, 0)]
            for slot in range(SLOTS):
                w_ext[slot] = w_ext[slot] - alpha * change[slot]
            z = add_coarse([w_ext[s] for s in range(SLOTS)], guess)
            for slot in range(SLOTS):
                p_ext[slot] = z[slot] + beta * p_ext[slot]
        else:
            own = full(jnp.sum(jnp.where(node == me, guess, 0.0), axis=0, keepdims=True))
            for x in range(MAIN):
                z_x = w_ext[x] - alpha * bq[x] + take(own, amaps[x])
                p_out[x] = z_x + beta * p_ext[x]
                r_out[x] = r_cur[x]


def emit(x_ref, r_ref, p_ref, x_out, r_out, p_out, sems):
    pairs = ((x_ref, x_out), (r_ref, r_out), (p_ref, p_out))
    copies = [pltpu.make_async_copy(a, b, sems.at[i]) for i, (a, b) in enumerate(pairs)]
    for copy in copies:
        copy.start()
    for copy in copies:
        copy.wait()


def shards(
    owners, members, right_side, coefficient_index, material_coefficients, block_cells,
    block_inverses, aggregate_map, coarse_diagonal,
):
    blocks, side = block_cells.shape[2], block_cells.shape[3]
    assert right_side.shape == (SUB, SUB, LANES) and side == LANES and blocks == SUB * SUB
    count = owners * members
    groups = blocks // SUB
    field = jax.ShapeDtypeStruct(right_side.shape, jnp.float32)
    vmem = pl.BlockSpec(memory_space=pltpu.VMEM)
    f32, i32 = jnp.float32, jnp.int32
    tile = (SUB, LANES)
    hbm = pl.BlockSpec(memory_space=pltpu.HBM)
    results = pl.pallas_call(
        functools.partial(kernel, owners, members),
        out_shape=(field, field, field),
        in_specs=[hbm] * 7,
        out_specs=(vmem, vmem, vmem),
        scratch_shapes=[
            pltpu.VMEM(right_side.shape, f32),
            pltpu.VMEM(right_side.shape, i32),
            pltpu.VMEM((1,) + material_coefficients.shape, f32),
            pltpu.VMEM((groups,) + tile, i32),
            pltpu.VMEM(right_side.shape, i32),
            pltpu.VMEM(coarse_diagonal.shape, f32),
            pltpu.SemaphoreType.DMA((6,)),
            pltpu.VMEM((blocks, side, side), f32),
            pltpu.VMEM((blocks, side, 2 * side), jnp.bfloat16),
            pltpu.VMEM((blocks,) + tile, f32),
            pltpu.VMEM((groups,) + tile, i32),
            pltpu.VMEM((groups,) + tile, i32),
            pltpu.VMEM((groups,) + tile, i32),
            pltpu.VMEM((groups,) + tile, i32),
            pltpu.VMEM((groups,) + tile, f32),
            pltpu.VMEM((CORNER, 3) + tile, f32),
            pltpu.VMEM((2, 3) + tile, f32),
            pltpu.VMEM((4,) + tile, f32),
            pltpu.VMEM((4,) + tile, f32),
            pltpu.VMEM((CORNER, 1) + tile, f32),
            pltpu.VMEM((2, 1) + tile, f32),
            pltpu.VMEM((4,) + tile, f32),
            pltpu.VMEM((4,) + tile, f32),
            pltpu.VMEM((SLOTS,) + tile, f32),
            pltpu.VMEM((SLOTS,) + tile, i32),
            pltpu.VMEM((SLOTS,) + tile, f32),
            pltpu.VMEM((SLOTS,) + tile, f32),
            pltpu.VMEM((MAIN,) + tile, f32),
            pltpu.VMEM((MAIN,) + tile, f32),
            pltpu.VMEM((MAIN,) + tile, f32),
            pltpu.VMEM((2,) + tile, f32),
            pltpu.VMEM((1 + ITERS, 1, LANES), f32),
            pltpu.VMEM((1 + ITERS, count, 1, LANES), f32),
            pltpu.SemaphoreType.DMA((groups,)),
            pltpu.SemaphoreType.DMA((ITERS, len(DIRECTIONS))),
            pltpu.SemaphoreType.DMA((ITERS, len(DIRECTIONS))),
            pltpu.SemaphoreType.DMA((1 + ITERS,)),
            pltpu.SemaphoreType.DMA((1 + ITERS,)),
        ],
        compiler_params=pltpu.CompilerParams(
            collective_id=0, has_side_effects=True, vmem_limit_bytes=32 << 20
        ),
    )(
        *(pltpu.with_memory_space_constraint(a, pltpu.HBM) for a in (
        right_side,
        coefficient_index,
        material_coefficients.reshape(1, -1),
        block_cells.reshape(groups, SUB, LANES),
        block_inverses.reshape(blocks, side, side),
        aggregate_map,
        coarse_diagonal,
        ))
    )
    return pl.pallas_call(
        emit,
        out_shape=(field, field, field),
        in_specs=[vmem] * 3,
        out_specs=(hbm,) * 3,
        scratch_shapes=[pltpu.SemaphoreType.DMA((3,))],
        compiler_params=pltpu.CompilerParams(vmem_limit_bytes=1 << 20),
    )(*results)


def solution(mesh):
    three = P("coarse", "fine", None)
    return jax.shard_map(
        functools.partial(shards, mesh.shape["coarse"], mesh.shape["fine"]),
        mesh=mesh,
        in_specs=(
            three,
            three,
            P(),
            P("coarse", "fine", None, None),
            P("coarse", "fine", None, None, None),
            three,
            three,
        ),
        out_specs=(three, three, three),
        check_vma=False,
    )
```
